128 devices in a mesh: ka: 8 (over y, z_hi), sy: 4 (over x), sz: 4 (over z_lo, core).
Axes of the slice: x: 4, y: 4, z: 4 (z_hi: 2, z_lo: 2; z = z_hi * 2 + z_lo), core: 2. Of those that a mesh axis runs over, the one named last changes fastest.
Arguments:
- orbitals: bfloat16 [16, 4, 2, 32, 128, 128], P('ka', None, None, 'sy', 'sz'), may hold values from -7.5 to 7.5
- coefficients: float32 [16, 4], replicated, may hold values from -4 to 4
- local_pot: float32 [32, 128, 128], P('sy', 'sz'), may hold values from 0 to 2
- perturb: float32 [32, 128, 128], P('sy', 'sz'), may hold values from -4 to 6
- q_index: int32 [1], replicated, may hold values from 0 to 1023
Outputs:
- responses: bfloat16 [16, 4, 2, 32, 128, 128], P('ka', None, None, 'sy', 'sz')
- density: float32 [32, 128, 128], P('sy', 'sz', 'ka')
The draws below stay inside these ranges and needn't reach their ends.
All inputs are finite; a program needn't handle non-finite values.
Results may differ from the reference program's by a relative error of at most 0.0035.
Values may be sent and summed in bfloat16 or wider, within the bound.
A program may use at most 64 MiB of HBM per device.

```python
import jax
import jax.numpy as jnp
from jax import lax

NX = 128
K_DEV = 2
BANDS = 4
ITERS = 3
KPTS = 16
NY = 32
NZ = 128
N_KA = 8


def draw_orbitals(key, part):
    shared_key = jax.random.fold_in(key, 11)
    own_key = jax.random.fold_in(key, 12)
    shared_shape = (1, BANDS, 2, NY, NZ, NX)
    own_shape = (KPTS, BANDS, 2, NY, NZ, NX)
    shared = jax.random.truncated_normal(shared_key, -5.0, 5.0, shared_shape, jnp.float32)
    own = jax.random.truncated_normal(own_key, -5.0, 5.0, own_shape, jnp.float32)
    return (0.70710678 * (shared + own)).astype(jnp.bfloat16)


def draw_perturb(key, part):
    noise_key = jax.random.fold_in(key, 21)
    row_ramp = jnp.arange(NY, dtype=jnp.float32)[:, None, None] / NY
    depth_ramp = jnp.arange(NZ, dtype=jnp.float32)[None, :, None] / NZ
    ramp = 0.5 * (row_ramp + depth_ramp)
    smooth = 0.25 + 1.5 * ramp
    noise = jax.random.truncated_normal(noise_key, -3.5, 3.5, (NY, NZ, NX), jnp.float32)
    return (smooth + noise).astype(jnp.float32)


def levels(key, shape, shards, low, top_value):
    gain, own = 1.0, jax.random.fold_in(key, 6)
    for axis_at, blocks in shards:
        heights = jnp.exp(jax.random.uniform(jax.random.fold_in(own, axis_at), (blocks,), jnp.float32, low / len(shards), top_value / len(shards)))
        gain = gain * jnp.repeat(heights, shape[axis_at] // blocks).reshape([-1 if axis == axis_at else 1 for axis in range(len(shape))])
    return gain


def gaussian(stream_key, extent, deviation, reach, kind=jnp.bfloat16):
    return jnp.clip(deviation * jax.random.normal(stream_key, extent, jnp.float32), -reach, reach).astype(kind)


def setup_inputs(seed: int = 0) -> dict:
    streams_of = jax.random.split(jax.random.key(seed), 6)
    orbitals = draw_orbitals(jax.random.fold_in(streams_of[5], 71), 0)
    coefficients = gaussian(streams_of[1], (KPTS, ITERS + 1), 1.0, 4.0, jnp.float32)
    local_pot = jnp.clip(2.0 * jax.random.uniform(streams_of[2], (NY, NZ, NX), jnp.float32) ** levels(streams_of[2], (NY, NZ, NX), ((0, 4), (1, 4)), -0.2, 0.2), 0.0, 2.0)
    perturb = draw_perturb(jax.random.fold_in(streams_of[5], 71), 0)
    q_index = jax.random.randint(streams_of[4], (1,), 0, 128 * N_KA).astype(jnp.int32)
    return {"orbitals": orbitals, "coefficients": coefficients, "local_pot": local_pot, "perturb": perturb, "q_index": q_index}


centre_weight = -7.5
near_weight = 4.0 / 3.0
far_weight = -1.0 / 12.0
norm_epsilon = 1e-6


def apply_scaled(values, local_pot):
    summed = centre_weight * values
    for offset, weight in ((1, near_weight), (2, far_weight)):
        for axis_number in (1, 2, 3):
            summed = summed + weight * (jnp.roll(values, offset, axis_number) + jnp.roll(values, -offset, axis_number))
    energy_applied = -0.5 * summed + local_pot * values
    return 0.2 * energy_applied - values


def expand(source, coeffs, local_pot):
    previous = source
    current = apply_scaled(source, local_pot)
    result = coeffs[0] * previous + coeffs[1] * current
    for order in range(2, ITERS + 1):
        following = 2.0 * apply_scaled(current, local_pot) - previous
        result = result + coeffs[order] * following
        previous = current
        current = following
    return result


def project(source, partner_set):
    flat_source = source.reshape((BANDS, 2, -1))
    flat_partner = partner_set.astype(jnp.float32).reshape((BANDS, 2, -1))
    source_re = flat_source[:, 0]
    source_im = flat_source[:, 1]
    partner_re = flat_partner[:, 0]
    partner_im = flat_partner[:, 1]
    highest = lax.Precision.HIGHEST
    intersection_re = jnp.einsum('bm,cm->bc', partner_re, source_re, precision=highest) + jnp.einsum('bm,cm->bc', partner_im, source_im, precision=highest)
    intersection_im = jnp.einsum('bm,cm->bc', partner_re, source_im, precision=highest) - jnp.einsum('bm,cm->bc', partner_im, source_re, precision=highest)
    norms = jnp.sum(partner_re * partner_re + partner_im * partner_im, axis=1)
    coef_re = intersection_re / (norms[:, None] + norm_epsilon)
    coef_im = intersection_im / (norms[:, None] + norm_epsilon)
    correct_re = jnp.einsum('bc,bm->cm', coef_re, partner_re, precision=highest) - jnp.einsum('bc,bm->cm', coef_im, partner_im, precision=highest)
    correct_im = jnp.einsum('bc,bm->cm', coef_im, partner_re, precision=highest) + jnp.einsum('bc,bm->cm', coef_re, partner_im, precision=highest)
    correction = jnp.stack([correct_re, correct_im], 1)
    return (flat_source - correction).reshape(source.shape)


def roll_groups(array, first_slot):
    grouped = array.reshape((N_KA, K_DEV) + array.shape[1:])
    doubled = jnp.concatenate([grouped, grouped], 0)
    moved = lax.dynamic_slice_in_dim(doubled, first_slot, N_KA, 0)
    return moved.reshape(array.shape)


def reference(orbitals, coefficients, local_pot, perturb, q_index):
    shift_count = (q_index[0].astype(jnp.int32) % N_KA).astype(jnp.int32)
    received = roll_groups(orbitals, ((N_KA - shift_count) % N_KA).astype(jnp.int32))

    def one_point(inputs):
        orbital_set, partner_set, coeffs = inputs
        source = perturb[None, None] * orbital_set.astype(jnp.float32)
        projected = project(source, partner_set)
        flat = projected.reshape((BANDS * 2, NY, NZ, NX))
        return expand(flat, coeffs, local_pot).astype(jnp.bfloat16).reshape(orbital_set.shape)

    answer = lax.map(one_point, (received, orbitals, coefficients))
    responses = roll_groups(answer, shift_count)

    def accumulate(carry, inputs):
        orbital_set, response_set = inputs
        term = jnp.sum(orbital_set.astype(jnp.float32) * response_set.astype(jnp.float32), axis=(0, 1))
        return carry + term, None

    zeros = jnp.zeros((NY, NZ, NX), jnp.float32)
    summed, unused = lax.scan(accumulate, zeros, (orbitals, responses))
    density = summed * (2.0 / KPTS)
    return responses, density
```

```python
import functools

import jax
import jax.numpy as jnp
from jax import lax
from jax.experimental import pallas as pl
from jax.experimental.pallas import tpu as pltpu
from jax.sharding import PartitionSpec as P

MESH = pl.DeviceIdType.MESH
F32 = jnp.float32
BF16 = jnp.bfloat16
HIGHEST = lax.Precision.HIGHEST

NEAR = 0.2 * -0.5 * 4.0 / 3.0
FAR = 0.2 * -0.5 * -1.0 / 12.0
EPSILON = 1e-6
BANDS = 4
GROUP = 4
PITCH = 40
LEAD = 8


def fold(value):
    return value[0:8] + value[8:16] + value[16:24] + value[24:32]


def kernel(
    shift, sizes, orb, coeffs, pot, pert, resp, dens,
    phi, part, potv, pertv, w_one, w_two, t0, t1, t2, accs, cf, outv, dacc,
    ysend, yrecv, zsend, zrecv, red_send, red_recv, dsend, drecv,
    load_sem, route_send, route_recv, red_s, red_r, halo_s, halo_r, out_sem, den_s, den_r,
):
    nka, nsy, nsz = sizes
    slots, fields, ny, nz, nx = phi.shape
    ka, sy, sz = lax.axis_index("ka"), lax.axis_index("sy"), lax.axis_index("sz")
    me = sy * nsz + sz

    def ka_at(step):
        return {"ka": lax.rem(ka + step, nka)}

    def group_at(step):
        return {"sy": lax.rem(sy + step // nsz, nsy), "sz": lax.rem(sz + step % nsz, nsz)}

    members = nsy * nsz
    loads = [
        pltpu.make_async_copy(orb, phi, load_sem.at[0]),
        pltpu.make_async_copy(pert, pertv, load_sem.at[1]),
        pltpu.make_async_copy(pot, potv, load_sem.at[2]),
    ]
    for copy in loads:
        copy.start()

    barrier = pltpu.get_barrier_semaphore()
    peers = [ka_at(d) for d in range(1, nka)] + [group_at(d) for d in range(1, members)]
    for peer in peers:
        pl.semaphore_signal(barrier, inc=1, device_id=peer, device_id_type=MESH)
    pl.semaphore_wait(barrier, len(peers))

    chunks = 4
    depth = ny // chunks
    routes = []
    for slot in range(slots):
        for j in range(chunks):
            src = orb.at[slot, :, pl.ds(j * depth, depth)]
            dst = part.at[slot, :, pl.ds(j * depth, depth)]
            at = slot * chunks + j
            if shift:
                routes.append(pltpu.make_async_remote_copy(
                    src, dst, route_send.at[at], route_recv.at[at],
                    device_id=ka_at(nka - shift), device_id_type=MESH,
                ))
            else:
                routes.append(pltpu.make_async_copy(src, dst, route_recv.at[at]))
    for copy in routes:
        copy.start()

    def arrived(at):
        if shift:
            routes[at].wait_recv()
        else:
            routes[at].wait()

    for copy in loads:
        copy.wait()
    w_one[...] = 0.2 * potv[...] - 0.25
    w_two[...] = 0.4 * potv[...] - 0.5
    dacc[...] = jnp.zeros_like(dacc)

    rows = accs.shape[0]
    lane = lax.broadcasted_iota(jnp.int32, (nx, rows), 0)
    entry = lax.shift_right_logical(lax.broadcasted_iota(jnp.int32, (nx, rows), 1), 3)
    norm_of = 32 + lax.shift_right_logical(jnp.bitwise_and(lane - 64, 15), 2)
    wanted = jnp.where(lane < 32, lane, jnp.where((lane >= 64) & (lane < 96), norm_of, -1))
    gather = jnp.where(wanted == entry, 1.0, 0.0).astype(F32)
    ones = jnp.ones((8, nx), F32)

    def inner(slot):
        accs[...] = jnp.zeros_like(accs)

        def plane(y, carry):
            pe = pertv[y]
            source = [
                (pe * phi[slot, 2 * c, y].astype(F32), pe * phi[slot, 2 * c + 1, y].astype(F32))
                for c in range(BANDS)
            ]
            for b in range(BANDS):
                p_re = part[slot, 2 * b, y].astype(F32)
                p_im = part[slot, 2 * b + 1, y].astype(F32)
                at = 8 * (32 + b)
                accs[at : at + 8] += fold(p_re * p_re + p_im * p_im)
                for c in range(BANDS):
                    s_re, s_im = source[c]
                    at = 8 * (b * BANDS + c)
                    accs[at : at + 8] += fold(p_re * s_re + p_im * s_im)
                    at += 8 * 16
                    accs[at : at + 8] += fold(p_re * s_im - p_im * s_re)
            return carry

        for j in range(chunks):
            arrived(slot * chunks + j)
            lax.fori_loop(j * depth, (j + 1) * depth, plane, 0)

    def red_copies(slot):
        return [
            pltpu.make_async_remote_copy(
                red_send.at[slot], red_recv.at[slot, me], red_s.at[slot, d], red_r.at[slot, d],
                device_id=group_at(d), device_id_type=MESH,
            )
            for d in range(1, members)
        ]

    def reduce_start(slot):
        by_entry = jnp.dot(gather, accs[...], precision=HIGHEST, preferred_element_type=F32)
        row = lax.dot_general(
            ones, by_entry, (((1,), (1,)), ((), ())), precision=HIGHEST, preferred_element_type=F32
        )
        red_send[slot] = row
        red_recv[slot, me] = row
        for copy in red_copies(slot):
            copy.start()

    def reduce_finish(slot):
        for copy in red_copies(slot):
            copy.wait()
        total = red_recv[slot, 0]
        for d in range(1, members):
            total = total + red_recv[slot, d]
        coef = total / (pltpu.roll(total, 64, 1) + EPSILON)
        for i in range(32):
            cf[i] = jnp.broadcast_to(coef[:, i : i + 1], (8, nx))

    def project(slot):
        def plane(y, carry):
            for half in range(nz // 16):
                at = pl.ds(16 * half, 16)

                def tiles(value):
                    return value.reshape(2, 8, nx)

                pe = tiles(pertv[y, at])
                partner = [tiles(part[slot, i, y, at].astype(F32)) for i in range(fields)]
                row = pl.ds(pl.multiple_of(LEAD + y * PITCH + 16 * half, 8), 16)
                for c in range(BANDS):
                    out_re = pe * tiles(phi[slot, 2 * c, y, at].astype(F32))
                    out_im = pe * tiles(phi[slot, 2 * c + 1, y, at].astype(F32))
                    for b in range(BANDS):
                        c_re = cf[b * BANDS + c]
                        c_im = cf[16 + b * BANDS + c]
                        p_re, p_im = partner[2 * b], partner[2 * b + 1]
                        out_re = out_re - (c_re * p_re - c_im * p_im)
                        out_im = out_im - (c_im * p_re + c_re * p_im)
                    t0[slot * fields + 2 * c, row] = out_re.reshape(16, nx)
                    t0[slot * fields + 2 * c + 1, row] = out_im.reshape(16, nx)
            return carry

        lax.fori_loop(0, ny, plane, 0)

    up_y = {"sy": lax.rem(sy + 1, nsy)}
    down_y = {"sy": lax.rem(sy + nsy - 1, nsy)}
    up_z = {"sz": lax.rem(sz + 1, nsz)}
    down_z = {"sz": lax.rem(sz + nsz - 1, nsz)}

    def halo_copies(e, g):
        at = pl.ds(g * GROUP, GROUP)
        sides = (
            (ysend, yrecv, 0, up_y), (ysend, yrecv, 1, down_y),
            (zsend, zrecv, 0, up_z), (zsend, zrecv, 1, down_z),
        )
        return [
            pltpu.make_async_remote_copy(
                out.at[e, side, at], into.at[e, side, at],
                halo_s.at[e, g, i], halo_r.at[e, g, i], device_id=peer, device_id_type=MESH,
            )
            for i, (out, into, side, peer) in enumerate(sides)
        ]

    def send(e, t, g):
        def field(f, carry):
            for i in range(2):
                first = LEAD + i * PITCH
                last = LEAD + (ny - 2 + i) * PITCH
                ysend[e, 0, f, i] = t[f, last : last + nz].astype(BF16)
                ysend[e, 1, f, i] = t[f, first : first + nz].astype(BF16)
            high = [t[f, pl.ds(LEAD + nz - 2 + i, ny, stride=PITCH)] for i in range(2)]
            low = [t[f, pl.ds(LEAD + i, ny, stride=PITCH)] for i in range(2)]
            zsend[e, 0, f] = jnp.concatenate(high, 0).astype(BF16)
            zsend[e, 1, f] = jnp.concatenate(low, 0).astype(BF16)
            return carry

        lax.fori_loop(g * GROUP, (g + 1) * GROUP, field, 0)
        for copy in halo_copies(e, g):
            copy.start()

    def applied(e, t, f, y, plane, w):
        first = LEAD + y * PITCH
        v = plane[y]
        near = plane[y + 1] + plane[y - 1]
        far = plane[y + 2] + plane[y - 2]
        near = near + (t[f, first + 1 : first + 1 + nz] + t[f, first - 1 : first - 1 + nz])
        far = far + (t[f, first + 2 : first + 2 + nz] + t[f, first - 2 : first - 2 + nz])
        near = near + (pltpu.roll(v, 1, 1) + pltpu.roll(v, nx - 1, 1))
        far = far + (pltpu.roll(v, 2, 1) + pltpu.roll(v, nx - 2, 1))
        scale = 1.0 if e == 0 else 2.0
        return w[y] * v + ((scale * NEAR) * near + (scale * FAR) * far)

    def step(e, g, slot):
        for copy in halo_copies(e, g):
            copy.wait()
        t = (t0, t1, t2)[e]
        if e == 2:
            row = lax.rem(ka + shift, nka) * slots + slot
            c0, c1, c2, c3 = (coeffs[row, j] for j in range(4))
            c13 = c1 - c3

        def field(f, carry):
            for side, start in ((0, LEAD - 2), (1, LEAD + nz)):
                rows_in = zrecv[e, side, f].astype(F32)
                t[f, pl.ds(start, ny, stride=PITCH)] = rows_in[0:ny]
                t[f, pl.ds(start + 1, ny, stride=PITCH)] = rows_in[ny : 2 * ny]
            plane = {}
            for y in range(ny):
                first = LEAD + y * PITCH
                plane[y] = t[f, first : first + nz]
            for i in range(2):
                plane[i - 2] = yrecv[e, 0, f, i].astype(F32)
                plane[ny + i] = yrecv[e, 1, f, i].astype(F32)
            for y in range(ny):
                at = slice(LEAD + y * PITCH, LEAD + y * PITCH + nz)
                if e == 0:
                    t1[f, at] = applied(e, t, f, y, plane, w_one)
                elif e == 1:
                    t2[f, at] = applied(e, t, f, y, plane, w_two) - t0[f, at]
                else:
                    doubled = applied(e, t, f, y, plane, w_two)
                    answer = (c0 * t0[f, at] + c13 * t1[f, at]) + (c2 * plane[y] + c3 * doubled)
                    rounded = answer.astype(BF16)
                    i = f - slot * fields
                    outv[slot, i, y] = rounded
                    dacc[y] += phi[slot, i, y].astype(F32) * rounded.astype(F32)
            return carry

        lax.fori_loop(g * GROUP, (g + 1) * GROUP, field, 0)

    def out_copy(g):
        slot, first = g * GROUP // fields, g * GROUP % fields
        at = pl.ds(first, GROUP)
        return pltpu.make_async_copy(outv.at[slot, at], resp.at[slot, at], out_sem.at[g])

    per_slot = fields // GROUP
    inner(0)
    reduce_start(0)
    for slot in range(slots):
        groups = range(slot * per_slot, (slot + 1) * per_slot)
        reduce_finish(slot)
        project(slot)
        for g in groups:
            send(0, t0, g)
        for g in groups:
            step(0, g, slot)
            send(1, t1, g)
        for g in groups:
            step(1, g, slot)
            send(2, t2, g)
        if slot + 1 < slots:
            inner(slot + 1)
            reduce_start(slot + 1)
        for g in groups:
            step(2, g, slot)
            out_copy(g).start()

    lanes = nx // nka
    lane_at = lax.broadcasted_iota(jnp.int32, (nz, nx), 1)
    scale = 2.0 / (slots * nka)
    for d in range(nka):
        for yg in range(ny // nka):
            packed = jnp.zeros((nz, nx), F32)
            for i in range(nka):
                moved = dacc[yg * nka + i]
                turn = (i - d) * lanes % nx
                if turn:
                    moved = pltpu.roll(moved, turn, 1)
                inside = (lane_at >= i * lanes) & (lane_at < (i + 1) * lanes)
                packed = jnp.where(inside, moved, packed)
            dsend[d, yg] = packed * scale
    den_copies = [
        pltpu.make_async_remote_copy(
            dsend.at[lax.rem(ka + d, nka)], drecv.at[d], den_s.at[d], den_r.at[d],
            device_id=ka_at(d), device_id_type=MESH,
        )
        for d in range(1, nka)
    ]
    for copy in den_copies:
        copy.start()
    for copy in den_copies:
        copy.wait()
    for yg in range(ny // nka):
        total = dsend[ka, yg]
        for d in range(1, nka):
            total = total + drecv[d, yg]
        for i in range(nka):
            moved = pltpu.roll(total, (nx - i * lanes) % nx, 1) if i else total
            dens[yg * nka + i] = moved[:, 0:lanes]

    for g in range(slots * per_slot):
        out_copy(g).wait()
    if shift:
        for copy in routes:
            copy.wait_send()


def call(shift, sizes, orb, coeffs, pot, pert):
    nka, nsy, nsz = sizes
    slots, fields, ny, nz, nx = orb.shape
    count = slots * fields
    groups = count // GROUP
    any_spec = pl.BlockSpec(memory_space=pl.ANY)
    dma = pltpu.SemaphoreType.DMA
    t_shape = (count, LEAD + ny * PITCH, nx)
    scratch = [
        pltpu.VMEM(orb.shape, BF16),
        pltpu.VMEM(orb.shape, BF16),
        pltpu.VMEM(pot.shape, F32),
        pltpu.VMEM(pot.shape, F32),
        pltpu.VMEM(pot.shape, F32),
        pltpu.VMEM(pot.shape, F32),
        pltpu.VMEM(t_shape, F32),
        pltpu.VMEM(t_shape, F32),
        pltpu.VMEM(t_shape, F32),
        pltpu.VMEM((40 * 8, nx), F32),
        pltpu.VMEM((32, 8, nx), F32),
        pltpu.VMEM(orb.shape, BF16),
        pltpu.VMEM(pot.shape, F32),
        pltpu.VMEM((3, 2, count, 2, nz, nx), BF16),
        pltpu.VMEM((3, 2, count, 2, nz, nx), BF16),
        pltpu.VMEM((3, 2, count, 2 * ny, nx), BF16),
        pltpu.VMEM((3, 2, count, 2 * ny, nx), BF16),
        pltpu.VMEM((slots, 8, nx), F32),
        pltpu.VMEM((slots, nsy * nsz, 8, nx), F32),
        pltpu.VMEM((nka, ny // nka, nz, nx), F32),
        pltpu.VMEM((nka, ny // nka, nz, nx), F32),
        dma((3,)),
        dma((slots * 4,)),
        dma((slots * 4,)),
        dma((slots, nsy * nsz)),
        dma((slots, nsy * nsz)),
        dma((3, groups, 4)),
        dma((3, groups, 4)),
        dma((groups,)),
        dma((nka,)),
        dma((nka,)),
    ]
    return pl.pallas_call(
        functools.partial(kernel, shift, sizes),
        out_shape=(
            jax.ShapeDtypeStruct(orb.shape, BF16),
            jax.ShapeDtypeStruct((ny, nz, nx // nka), F32),
        ),
        in_specs=[any_spec, pl.BlockSpec(memory_space=pltpu.SMEM), any_spec, any_spec],
        out_specs=(any_spec, pl.BlockSpec(memory_space=pltpu.VMEM)),
        scratch_shapes=scratch,
        compiler_params=pltpu.CompilerParams(
            collective_id=shift, has_side_effects=True, vmem_limit_bytes=48 << 20
        ),
        name=f"respond_{shift}",
    )(orb, coeffs, pot, pert)


def body(sizes, orbitals, coefficients, local_pot, perturb, q_index):
    nka = sizes[0]
    slots = orbitals.shape[0]
    orb = orbitals.reshape((slots, -1) + orbitals.shape[3:])
    shift = q_index[0] % nka
    branches = [functools.partial(call, s, sizes) for s in range(nka)]
    responses, density = lax.switch(shift, branches, orb, coefficients, local_pot, perturb)
    return responses.reshape(orbitals.shape), density


def solution(mesh):
    sizes = (mesh.shape["ka"], mesh.shape["sy"], mesh.shape["sz"])
    return jax.shard_map(
        functools.partial(body, sizes),
        mesh=mesh,
        in_specs=(
            P("ka", None, None, "sy", "sz", None),
            P(),
            P("sy", "sz", None),
            P("sy", "sz", None),
            P(),
        ),
        out_specs=(P("ka", None, None, "sy", "sz", None), P("sy", "sz", "ka")),
        check_vma=False,
    )
```

```python
import functools

import jax
import jax.numpy as jnp
from jax import lax
from jax.experimental import pallas as pl
from jax.experimental.pallas import tpu as pltpu
from jax.sharding import PartitionSpec as P

MESH = pl.DeviceIdType.MESH
F32 = jnp.float32
BF16 = jnp.bfloat16

UNIT = 0.2 * 0.5 / 12.0
EPSILON = 1e-6
BANDS = 4
GROUP = 4
PITCH = 40
LEAD = 8


def fold(value):
    return value[0:8] + value[8:16] + value[16:24] + value[24:32]


def kernel(
    sizes, q_ref, orb, coeffs, pot, pert, resp, dens,
    phi, mid_a, mid_b, stage, land_a, land_b, potv, pertv, w_one, w_two, ring, t0, t1, t2, accs, entries, cf, dacc,
    ysend, yrecv, zsend, zrecv, red_send, red_recv, dsend, drecv,
    load_sem, first_s, first_r, second_s, second_r, red_s, red_r, halo_s, halo_r, den_s, den_r,
):
    nka, nsy, nsz = sizes
    slots, fields, ny, nz, nx = phi.shape
    ka, sy, sz = lax.axis_index("ka"), lax.axis_index("sy"), lax.axis_index("sz")

    def ka_at(step):
        return {"ka": lax.rem(ka + step, nka)}

    def group_at(step):
        return {"sy": lax.rem(sy + step // nsz, nsy), "sz": lax.rem(sz + step % nsz, nsz)}

    members = nsy * nsz
    mids, lands = (mid_a, mid_b), (land_a, land_b)
    loads = [
        pltpu.make_async_copy(orb, phi, load_sem.at[0]),
        pltpu.make_async_copy(pert, pertv, load_sem.at[1]),
        pltpu.make_async_copy(pot, potv, load_sem.at[2]),
    ]
    for copy in loads:
        copy.start()

    barrier = pltpu.get_barrier_semaphore()
    peers = [ka_at(d) for d in range(1, nka)] + [group_at(d) for d in range(1, members)]
    for peer in peers:
        pl.semaphore_signal(barrier, inc=1, device_id=peer, device_id_type=MESH)
    pl.semaphore_wait(barrier, len(peers))

    def awaited(ref, sem):
        return pltpu.make_async_copy(ref, ref, sem)

    def routed(src, dst, send, recv):
        return [
            pltpu.make_async_remote_copy(
                src.at[d], dst.at[d], send, recv, device_id=ka_at(d), device_id_type=MESH
            )
            for d in range(1, nka)
        ]

    def piece(of):
        return jnp.bitwise_and(-q_ref[0] - of, nka - 1)

    for slot in range(slots):
        for copy in routed(orb.at[slot], mids[slot], first_s.at[slot], first_r.at[slot]):
            copy.start()

    for copy in loads:
        copy.wait()
    w_one[...] = 0.2 * potv[...] - 0.25
    w_two[...] = 0.4 * potv[...] - 0.5
    dacc[...] = jnp.zeros_like(dacc)

    row_at = lax.broadcasted_iota(jnp.int32, (nx, nx), 0)
    column_at = lax.broadcasted_iota(jnp.int32, (nx, nx), 1)
    apart = jnp.bitwise_and(row_at - column_at, nx - 1)
    circle = jnp.where(
        (apart == 1) | (apart == nx - 1), -16.0, jnp.where((apart == 2) | (apart == nx - 2), 1.0, 0.0)
    ).astype(BF16)
    ring[0:nx] = circle
    ring[nx : 2 * nx] = circle
    ones = jnp.ones((8, nx), BF16)
    entries[...] = jnp.zeros_like(entries)

    for slot in range(slots):
        mid, land = mids[slot], lands[slot]
        mid[0] = phi[slot, 0]
        awaited(mid.at[1:nka], first_r.at[slot]).wait()
        land[0] = mid[piece(0)]
        for d in range(1, nka):
            stage[slot, d] = mid[piece(d)]
        for copy in routed(stage.at[slot], land, second_s.at[slot], second_r.at[slot]):
            copy.start()

    def inner(slot):
        accs[...] = jnp.zeros_like(accs)

        def plane(y, carry):
            pe = pertv[y]
            source = [
                (pe * phi[slot, 2 * c, y].astype(F32), pe * phi[slot, 2 * c + 1, y].astype(F32))
                for c in range(BANDS)
            ]
            for b in range(BANDS):
                p_re = lands[slot][piece(2 * b), y].astype(F32)
                p_im = lands[slot][piece(2 * b + 1), y].astype(F32)
                at = 8 * (32 + b)
                accs[at : at + 8] += fold(p_re * p_re + p_im * p_im)
                for c in range(BANDS):
                    s_re, s_im = source[c]
                    at = 8 * (b * BANDS + c)
                    accs[at : at + 8] += fold(p_re * s_re + p_im * s_im)
                    at += 8 * 16
                    accs[at : at + 8] += fold(p_re * s_im - p_im * s_re)
            return carry

        awaited(lands[slot].at[1:nka], second_r.at[slot]).wait()
        lax.fori_loop(0, ny, plane, 0)

    def reduce_start(slot):
        count = 32 + BANDS
        summed = accs[pl.ds(0, count, stride=8)]
        for i in range(1, 8):
            summed = summed + accs[pl.ds(i, count, stride=8)]
        entries[0:32] = summed[0:32]
        for b in range(BANDS):
            norm = jnp.broadcast_to(summed[32 + b : 33 + b], (BANDS, nx))
            entries[64 + b * BANDS : 64 + (b + 1) * BANDS] = norm
            entries[80 + b * BANDS : 80 + (b + 1) * BANDS] = norm
        whole = entries[...]
        row = jnp.zeros((8, nx), F32)
        for _ in range(3):
            rounded = whole.astype(BF16)
            row = row + lax.dot_general(
                ones, rounded, (((1,), (1,)), ((), ())), preferred_element_type=F32
            )
            whole = whole - rounded.astype(F32)
        for d in range(members):
            red_send[slot, d] = row
        for d in range(1, members):
            pltpu.make_async_remote_copy(
                red_send.at[slot, d], red_recv.at[slot, d], red_s.at[slot], red_r.at[slot],
                device_id=group_at(d), device_id_type=MESH,
            ).start()

    def reduce_finish(slot):
        awaited(red_recv.at[slot, 1:members], red_r.at[slot]).wait()
        total = red_send[slot, 0]
        for d in range(1, members):
            total = total + red_recv[slot, d]
        coef = total / (pltpu.roll(total, 64, 1) + EPSILON)
        for i in range(32):
            cf[i] = jnp.broadcast_to(coef[:, i : i + 1], (8, nx))

    def project(slot):
        def plane(y, carry):
            for half in range(nz // 16):
                at = pl.ds(16 * half, 16)

                def tiles(value):
                    return value.reshape(2, 8, nx)

                pe = tiles(pertv[y, at])
                partner = [tiles(lands[slot][piece(i), y, at].astype(F32)) for i in range(fields)]
                row = pl.ds(pl.multiple_of(LEAD + y * PITCH + 16 * half, 8), 16)
                for c in range(BANDS):
                    out_re = pe * tiles(phi[slot, 2 * c, y, at].astype(F32))
                    out_im = pe * tiles(phi[slot, 2 * c + 1, y, at].astype(F32))
                    for b in range(BANDS):
                        c_re = cf[b * BANDS + c]
                        c_im = cf[16 + b * BANDS + c]
                        p_re, p_im = partner[2 * b], partner[2 * b + 1]
                        out_re = out_re - (c_re * p_re - c_im * p_im)
                        out_im = out_im - (c_im * p_re + c_re * p_im)
                    t0[slot * fields + 2 * c, row] = out_re.reshape(16, nx)
                    t0[slot * fields + 2 * c + 1, row] = out_im.reshape(16, nx)
            return carry

        lax.fori_loop(0, ny, plane, 0)

    up_y = {"sy": lax.rem(sy + 1, nsy)}
    down_y = {"sy": lax.rem(sy + nsy - 1, nsy)}
    up_z = {"sz": lax.rem(sz + 1, nsz)}
    down_z = {"sz": lax.rem(sz + nsz - 1, nsz)}

    def halo_copies(e, g):
        at = pl.ds(g * GROUP, GROUP)
        sides = (
            (ysend, yrecv, 0, up_y, 0), (ysend, yrecv, 1, down_y, 0),
            (zsend, zrecv, 0, up_z, 1), (zsend, zrecv, 1, down_z, 1),
        )
        return [
            pltpu.make_async_remote_copy(
                out.at[e, side, at], into.at[e, side, at],
                halo_s.at[e, g, i], halo_r.at[e, g, i], device_id=peer, device_id_type=MESH,
            )
            for out, into, side, peer, i in sides
        ]

    def send(e, t, g):
        def field(f, carry):
            for i in range(2):
                first = LEAD + i * PITCH
                last = LEAD + (ny - 2 + i) * PITCH
                ysend[e, 0, f, i] = t[f, last : last + nz].astype(BF16)
                ysend[e, 1, f, i] = t[f, first : first + nz].astype(BF16)
            high = [t[f, pl.ds(LEAD + nz - 2 + i, ny, stride=PITCH)] for i in range(2)]
            low = [t[f, pl.ds(LEAD + i, ny, stride=PITCH)] for i in range(2)]
            zsend[e, 0, f] = jnp.concatenate(high, 0).astype(BF16)
            zsend[e, 1, f] = jnp.concatenate(low, 0).astype(BF16)
            return carry

        lax.fori_loop(g * GROUP, (g + 1) * GROUP, field, 0)
        for copy in halo_copies(e, g):
            copy.start()

    def applied(e, t, f, y, plane, along_x, w):
        first = LEAD + y * PITCH
        near = plane[y + 1] + plane[y - 1]
        far = plane[y + 2] + plane[y - 2]
        near = near + (t[f, first + 1 : first + 1 + nz] + t[f, first - 1 : first - 1 + nz])
        far = far + (t[f, first + 2 : first + 2 + nz] + t[f, first - 2 : first - 2 + nz])
        unit = UNIT if e == 0 else 2.0 * UNIT
        return w[y] * plane[y] + unit * ((far + along_x[y * nz : (y + 1) * nz]) - 16.0 * near)

    def step(e, g, slot):
        at = pl.ds(g * GROUP, GROUP)
        for i, ref in enumerate((yrecv, zrecv)):
            awaited(ref.at[e, :, at], halo_r.at[e, g, i]).wait()
        t = (t0, t1, t2)[e]
        if e == 2:
            row = jnp.bitwise_and(ka + q_ref[0], nka - 1) * slots + slot
            c0, c1, c2, c3 = (coeffs[j, row] for j in range(4))
            c13 = c1 - c3

        def field(f, carry):
            for side, start in ((0, LEAD - 2), (1, LEAD + nz)):
                rows_in = zrecv[e, side, f].astype(F32)
                t[f, pl.ds(start, ny, stride=PITCH)] = rows_in[0:ny]
                t[f, pl.ds(start + 1, ny, stride=PITCH)] = rows_in[ny : 2 * ny]
            plane = {}
            for y in range(ny):
                first = LEAD + y * PITCH
                plane[y] = t[f, first : first + nz]
            whole = jnp.concatenate([plane[y] for y in range(ny)], 0)
            high = whole.astype(BF16)
            low = (whole - high.astype(F32)).astype(BF16)
            along_x = jnp.dot(
                jnp.concatenate([high, low], 1), ring[...], preferred_element_type=F32
            )
            for i in range(2):
                plane[i - 2] = yrecv[e, 0, f, i].astype(F32)
                plane[ny + i] = yrecv[e, 1, f, i].astype(F32)
            for y in range(ny):
                at = slice(LEAD + y * PITCH, LEAD + y * PITCH + nz)
                if e == 0:
                    t1[f, at] = applied(e, t, f, y, plane, along_x, w_one)
                elif e == 1:
                    t2[f, at] = applied(e, t, f, y, plane, along_x, w_two) - t0[f, at]
                else:
                    doubled = applied(e, t, f, y, plane, along_x, w_two)
                    answer = (c0 * t0[f, at] + c13 * t1[f, at]) + (c2 * plane[y] + c3 * doubled)
                    rounded = answer.astype(BF16)
                    i = f - slot * fields
                    resp[slot, i, y] = rounded
                    dacc[y] += phi[slot, i, y].astype(F32) * rounded.astype(F32)
            return carry

        lax.fori_loop(g * GROUP, (g + 1) * GROUP, field, 0)

    def groups(slot):
        per_slot = fields // GROUP
        return range(slot * per_slot, (slot + 1) * per_slot)

    def begin(slot):
        inner(slot)
        reduce_start(slot)

    def start_expansion(slot):
        reduce_finish(slot)
        project(slot)
        for g in groups(slot):
            send(0, t0, g)

    def advance(slot, e):
        for g in groups(slot):
            step(e, g, slot)
            if e == 0:
                send(1, t1, g)
            elif e == 1:
                send(2, t2, g)

    begin(0)
    start_expansion(0)
    begin(1)
    advance(0, 0)
    start_expansion(1)
    advance(0, 1)
    advance(1, 0)
    advance(0, 2)
    advance(1, 1)
    advance(1, 2)

    lanes = nx // nka
    lane_at = lax.broadcasted_iota(jnp.int32, (nz, nx), 1)
    scale = 2.0 / (slots * nka)
    block_at = lax.shift_right_logical(lane_at, lanes.bit_length() - 1)
    blocks = [dacc[y] * scale for y in range(ny)]
    stride = nka // 2
    while stride:
        odd = jnp.bitwise_and(block_at, stride) != 0
        for i in range(nka):
            if not i & stride:
                one, two = blocks[i], blocks[i + stride]
                blocks[i] = jnp.where(odd, pltpu.roll(two, stride * lanes, 1), one)
                blocks[i + stride] = jnp.where(odd, two, pltpu.roll(one, nx - stride * lanes, 1))
        stride //= 2
    for d in range(nka):
        dsend[d] = blocks[d]
    den_copies = [
        pltpu.make_async_remote_copy(
            dsend.at[lax.rem(ka + d, nka)], drecv.at[d], den_s, den_r,
            device_id=ka_at(d), device_id_type=MESH,
        )
        for d in range(1, nka)
    ]
    for copy in den_copies:
        copy.start()
    awaited(drecv.at[1:nka], den_r).wait()
    total = dsend[ka]
    for d in range(1, nka):
        total = total + drecv[d]
    dens[...] = jnp.transpose(total)

    awaited(dsend.at[1:nka], den_s).wait()
    for slot in range(slots):
        awaited(orb.at[slot, 1:nka], first_s.at[slot]).wait()
        awaited(stage.at[slot, 1:nka], second_s.at[slot]).wait()
        awaited(red_send.at[slot, 1:members], red_s.at[slot]).wait()
    for e in range(3):
        for g in range(slots * fields // GROUP):
            at = pl.ds(g * GROUP, GROUP)
            awaited(ysend.at[e, :, at], halo_s.at[e, g, 0]).wait()
            awaited(zsend.at[e, :, at], halo_s.at[e, g, 1]).wait()


def call(sizes, q_index, orb, coeffs, pot, pert):
    nka, nsy, nsz = sizes
    slots, fields, ny, nz, nx = orb.shape
    count = slots * fields
    groups = count // GROUP
    hbm = pl.BlockSpec(memory_space=pltpu.HBM)
    smem = pl.BlockSpec(memory_space=pltpu.SMEM)
    vmem = pl.BlockSpec(memory_space=pltpu.VMEM)
    dma = pltpu.SemaphoreType.DMA
    t_shape = (count, LEAD + ny * PITCH, nx)
    scratch = [
        pltpu.VMEM(orb.shape, BF16),
        pltpu.VMEM(orb.shape[1:], BF16),
        pltpu.VMEM(orb.shape[1:], BF16),
        pltpu.VMEM(orb.shape, BF16),
        pltpu.VMEM(orb.shape[1:], BF16),
        pltpu.VMEM(orb.shape[1:], BF16),
        pltpu.VMEM(pot.shape, F32),
        pltpu.VMEM(pot.shape, F32),
        pltpu.VMEM(pot.shape, F32),
        pltpu.VMEM(pot.shape, F32),
        pltpu.VMEM((2 * nx, nx), BF16),
        pltpu.VMEM(t_shape, F32),
        pltpu.VMEM(t_shape, F32),
        pltpu.VMEM(t_shape, F32),
        pltpu.VMEM((40 * 8, nx), F32),
        pltpu.VMEM((nx, nx), F32),
        pltpu.VMEM((32, 8, nx), F32),
        pltpu.VMEM(pot.shape, F32),
        pltpu.VMEM((3, 2, count, 2, nz, nx), BF16),
        pltpu.VMEM((3, 2, count, 2, nz, nx), BF16),
        pltpu.VMEM((3, 2, count, 2 * ny, nx), BF16),
        pltpu.VMEM((3, 2, count, 2 * ny, nx), BF16),
        pltpu.VMEM((slots, nsy * nsz, 8, nx), F32),
        pltpu.VMEM((slots, nsy * nsz, 8, nx), F32),
        pltpu.VMEM((nka, nz, nx), F32),
        pltpu.VMEM((nka, nz, nx), F32),
        dma((3,)),
        dma((slots,)),
        dma((slots,)),
        dma((slots,)),
        dma((slots,)),
        dma((slots,)),
        dma((slots,)),
        dma((3, groups, 2)),
        dma((3, groups, 2)),
        dma,
        dma,
    ]
    held = [pltpu.with_memory_space_constraint(x, pltpu.HBM) for x in (orb, pot, pert)]
    return pl.pallas_call(
        functools.partial(kernel, sizes),
        out_shape=(
            pltpu.VMEM(orb.shape, BF16),
            pltpu.VMEM((nx, nz), F32),
        ),
        in_specs=[smem, hbm, smem, hbm, hbm],
        out_specs=(vmem, vmem),
        scratch_shapes=scratch,
        compiler_params=pltpu.CompilerParams(
            collective_id=0, has_side_effects=True, vmem_limit_bytes=48 << 20
        ),
        name="respond",
    )(q_index, *held[:1], coeffs, *held[1:])


def body(sizes, orbitals, coefficients, local_pot, perturb, q_index):
    orb = orbitals.reshape((orbitals.shape[0], -1) + orbitals.shape[3:])
    responses, density = call(sizes, q_index, orb, coefficients.T, local_pot, perturb)
    ny, nz, nx = local_pot.shape
    density = density.reshape((ny, nx // sizes[0], nz)).transpose(0, 2, 1)
    return responses.reshape(orbitals.shape), density


def solution(mesh):
    sizes = (mesh.shape["ka"], mesh.shape["sy"], mesh.shape["sz"])
    return jax.shard_map(
        functools.partial(body, sizes),
        mesh=mesh,
        in_specs=(
            P("ka", None, None, "sy", "sz", None),
            P(),
            P("sy", "sz", None),
            P("sy", "sz", None),
            P(),
        ),
        out_specs=(P("ka", None, None, "sy", "sz", None), P("sy", "sz", "ka")),
        check_vma=False,
    )
```

```python
import functools

import jax
import jax.numpy as jnp
from jax import lax
from jax.experimental import pallas as pl
from jax.experimental.pallas import tpu as pltpu
from jax.sharding import PartitionSpec as P

MESH = pl.DeviceIdType.MESH
F32 = jnp.float32
BF16 = jnp.bfloat16

UNIT = 0.2 * 0.5 / 12.0
EPSILON = 1e-6
BANDS = 4
GROUP = 4
PITCH = 40
LEAD = 8


def fold(value):
    return value[0:8] + value[8:16] + value[16:24] + value[24:32]


def kernel(
    sizes, q_ref, orb, coeffs_in, pot, pert, resp, dens,
    coeffs, phi, mid_a, mid_b, stage, land_a, land_b, potv, pertv, w_one, w_two, ring, t0, t1, t2, accs, entries, cf, dacc,
    phi_y, phi_z, phi_zs, pert_y, pert_z, pert_zs, part_y_a, part_y_b, part_z_a, part_z_b, part_zs, zpack,
    ysend, yrecv, zsend, zrecv, red_send, red_recv, dsend, drecv,
    load_sem, first_s, first_r, second_s, second_r, red_s, red_r, early_s, early_r, halo_s, halo_r, den_s, den_r,
):
    nka, nsy, nsz = sizes
    slots, fields, ny, nz, nx = phi.shape
    ka, sy, sz = lax.axis_index("ka"), lax.axis_index("sy"), lax.axis_index("sz")

    def ka_at(step):
        return {"ka": lax.rem(ka + step, nka)}

    def group_at(step):
        return {"sy": lax.rem(sy + step // nsz, nsy), "sz": lax.rem(sz + step % nsz, nsz)}

    members = nsy * nsz
    mids, lands = (mid_a, mid_b), (land_a, land_b)
    parts_y, parts_z = (part_y_a, part_y_b), (part_z_a, part_z_b)
    loads = [
        pltpu.make_async_copy(orb, phi, load_sem.at[0]),
        pltpu.make_async_copy(pert, pertv, load_sem.at[1]),
        pltpu.make_async_copy(pot, potv, load_sem.at[2]),
        pltpu.make_async_copy(coeffs_in, coeffs, load_sem.at[3]),
    ]
    for copy in loads:
        copy.start()

    barrier = pltpu.get_barrier_semaphore()
    peers = [ka_at(d) for d in range(1, nka)] + [group_at(d) for d in range(1, members)]
    for peer in peers:
        pl.semaphore_signal(barrier, inc=1, device_id=peer, device_id_type=MESH)
    pl.semaphore_wait(barrier, len(peers))

    up_y = {"sy": lax.rem(sy + 1, nsy)}
    down_y = {"sy": lax.rem(sy + nsy - 1, nsy)}
    up_z = {"sz": lax.rem(sz + 1, nsz)}
    down_z = {"sz": lax.rem(sz + nsz - 1, nsz)}

    def early(i, high, low, into, peers):
        for src, side, peer in ((high, 0, peers[0]), (low, 1, peers[1])):
            pltpu.make_async_remote_copy(
                src, into.at[side], early_s.at[i], early_r.at[i], device_id=peer, device_id_type=MESH
            ).start()

    along_y, along_z = (up_y, down_y), (up_z, down_z)

    def pack_z(read):
        zpack[...] = read(slice(nz - 8, nz)).astype(F32).reshape(8 * ny, nx)
        high = [zpack[pl.ds(6 + i, ny, stride=8)] for i in range(2)]
        zpack[...] = read(slice(0, 8)).astype(F32).reshape(8 * ny, nx)
        low = [zpack[pl.ds(i, ny, stride=8)] for i in range(2)]
        return jnp.concatenate(high, 0), jnp.concatenate(low, 0)

    def awaited(ref, sem):
        return pltpu.make_async_copy(ref, ref, sem)

    def routed(src, dst, send, recv):
        return [
            pltpu.make_async_remote_copy(
                src.at[d], dst.at[d], send, recv, device_id=ka_at(d), device_id_type=MESH
            )
            for d in range(1, nka)
        ]

    def piece(of):
        return jnp.bitwise_and(-q_ref[0] - of, nka - 1)

    for slot in range(slots):
        for copy in routed(orb.at[slot], mids[slot], first_s.at[slot], first_r.at[slot]):
            copy.start()

    for slot in range(slots):
        early(slot, orb.at[slot, :, ny - 2 : ny], orb.at[slot, :, 0:2], phi_y.at[slot], along_y)
    early(2, pert.at[ny - 2 : ny], pert.at[0:2], pert_y, along_y)
    for copy in loads:
        copy.wait()
    for slot in range(slots):

        def own_field(i, carry):
            high, low = pack_z(lambda at: phi[slot, i, :, at])
            phi_zs[0, slot, i] = high.astype(BF16)
            phi_zs[1, slot, i] = low.astype(BF16)
            return carry

        lax.fori_loop(0, fields, own_field, 0)
    pert_zs[0], pert_zs[1] = pack_z(lambda at: pertv[:, at])
    early(3, phi_zs.at[0], phi_zs.at[1], phi_z, along_z)
    early(4, pert_zs.at[0], pert_zs.at[1], pert_z, along_z)
    w_one[...] = 0.2 * potv[...] - 0.25
    w_two[...] = 0.4 * potv[...] - 0.5
    dacc[...] = jnp.zeros_like(dacc)

    row_at = lax.broadcasted_iota(jnp.int32, (nx, nx), 0)
    column_at = lax.broadcasted_iota(jnp.int32, (nx, nx), 1)
    apart = jnp.bitwise_and(row_at - column_at, nx - 1)
    circle = jnp.where(
        (apart == 1) | (apart == nx - 1), -16.0, jnp.where((apart == 2) | (apart == nx - 2), 1.0, 0.0)
    ).astype(BF16)
    ring[0:nx] = circle
    ring[nx : 2 * nx] = circle
    ones = jnp.ones((8, nx), BF16)
    entries[...] = jnp.zeros_like(entries)

    for slot in range(slots):
        mid, land = mids[slot], lands[slot]
        mid[0] = phi[slot, 0]
        awaited(mid.at[1:nka], first_r.at[slot]).wait()
        land[0] = mid[piece(0)]
        for d in range(1, nka):
            stage[slot, d] = mid[piece(d)]
        for copy in routed(stage.at[slot], land, second_s.at[slot], second_r.at[slot]):
            copy.start()

    def inner(slot):
        accs[...] = jnp.zeros_like(accs)

        def plane(y, carry):
            pe = pertv[y]
            source = [
                (pe * phi[slot, 2 * c, y].astype(F32), pe * phi[slot, 2 * c + 1, y].astype(F32))
                for c in range(BANDS)
            ]
            for b in range(BANDS):
                p_re = lands[slot][piece(2 * b), y].astype(F32)
                p_im = lands[slot][piece(2 * b + 1), y].astype(F32)
                at = 8 * (32 + b)
                accs[at : at + 8] += fold(p_re * p_re + p_im * p_im)
                for c in range(BANDS):
                    s_re, s_im = source[c]
                    at = 8 * (b * BANDS + c)
                    accs[at : at + 8] += fold(p_re * s_re + p_im * s_im)
                    at += 8 * 16
                    accs[at : at + 8] += fold(p_re * s_im - p_im * s_re)
            return carry

        awaited(lands[slot].at[1:nka], second_r.at[slot]).wait()
        land = lands[slot]
        early(5 + slot, land.at[:, ny - 2 : ny], land.at[:, 0:2], parts_y[slot], along_y)
        lax.fori_loop(0, ny, plane, 0)

    def reduce_start(slot):
        count = 32 + BANDS
        summed = accs[pl.ds(0, count, stride=8)]
        for i in range(1, 8):
            summed = summed + accs[pl.ds(i, count, stride=8)]
        entries[0:32] = summed[0:32]
        for b in range(BANDS):
            norm = jnp.broadcast_to(summed[32 + b : 33 + b], (BANDS, nx))
            entries[64 + b * BANDS : 64 + (b + 1) * BANDS] = norm
            entries[80 + b * BANDS : 80 + (b + 1) * BANDS] = norm
        whole = entries[...]
        row = jnp.zeros((8, nx), F32)
        for _ in range(3):
            rounded = whole.astype(BF16)
            row = row + lax.dot_general(
                ones, rounded, (((1,), (1,)), ((), ())), preferred_element_type=F32
            )
            whole = whole - rounded.astype(F32)
        red_send[slot] = row[0:1]
        for d in range(1, members):
            pltpu.make_async_remote_copy(
                red_send.at[slot], red_recv.at[slot, d], red_s.at[slot], red_r.at[slot],
                device_id=group_at(d), device_id_type=MESH,
            ).start()

    def reduce_finish(slot):
        awaited(red_recv.at[slot, 1:members], red_r.at[slot]).wait()
        total = red_send[slot]
        for d in range(1, members):
            total = total + red_recv[slot, d]
        coef = total / (pltpu.roll(total, 64, 1) + EPSILON)
        for i in range(32):
            cf[i] = jnp.broadcast_to(coef[:, i : i + 1], (8, nx))

    def partner_z(slot):
        def field(i, carry):
            high, low = pack_z(lambda at: lands[slot][i, :, at])
            part_zs[slot, 0, i] = high.astype(BF16)
            part_zs[slot, 1, i] = low.astype(BF16)
            return carry

        lax.fori_loop(0, fields, field, 0)
        early(7 + slot, part_zs.at[slot, 0], part_zs.at[slot, 1], parts_z[slot], along_z)

    def projected(pe, own, partner):
        def tiles(value):
            return value.astype(F32).reshape(2, 8, nx)

        pe = tiles(pe)
        partner = [tiles(value) for value in partner]
        out = []
        for c in range(BANDS):
            out_re = pe * tiles(own[2 * c])
            out_im = pe * tiles(own[2 * c + 1])
            for b in range(BANDS):
                c_re = cf[b * BANDS + c]
                c_im = cf[16 + b * BANDS + c]
                p_re, p_im = partner[2 * b], partner[2 * b + 1]
                out_re = out_re - (c_re * p_re - c_im * p_im)
                out_im = out_im - (c_im * p_re + c_re * p_im)
            out += [out_re.reshape(16, nx), out_im.reshape(16, nx)]
        return out

    def project(slot):
        every = range(fields)
        land, part_y, part_z = lands[slot], parts_y[slot], parts_z[slot]
        first_field = slot * fields

        def plane(y, carry):
            for half in range(nz // 16):
                at = pl.ds(16 * half, 16)
                row = pl.ds(pl.multiple_of(LEAD + y * PITCH + 16 * half, 8), 16)
                out = projected(
                    pertv[y, at],
                    [phi[slot, i, y, at] for i in every],
                    [land[piece(i), y, at] for i in every],
                )
                for i in every:
                    t0[first_field + i, row] = out[i]
            return carry

        lax.fori_loop(0, ny, plane, 0)

        def outer_plane(i, carry):
            side, layer = lax.shift_right_logical(i, 1), jnp.bitwise_and(i, 1)
            for half in range(nz // 16):
                at = pl.ds(16 * half, 16)
                out = projected(
                    pert_y[side, layer, at],
                    [phi_y[slot, side, f, layer, at] for f in every],
                    [part_y[side, piece(f), layer, at] for f in every],
                )
                for f in every:
                    yrecv[0, side, first_field + f, layer, at] = out[f].astype(BF16)
            return carry

        def outer_rows(side, carry):
            out = projected(
                pert_z[side],
                [phi_z[side, slot, f] for f in every],
                [part_z[side, piece(f)] for f in every],
            )
            for f in every:
                zrecv[0, side, first_field + f] = out[f].astype(BF16)
            return carry

        awaited(part_y, early_r.at[5 + slot]).wait()
        awaited(part_z, early_r.at[7 + slot]).wait()
        lax.fori_loop(0, 4, outer_plane, 0)
        lax.fori_loop(0, 2, outer_rows, 0)

    def halo_copies(e, g):
        at = pl.ds(g * GROUP, GROUP)
        sides = (
            (ysend, yrecv, 0, up_y, 0), (ysend, yrecv, 1, down_y, 0),
            (zsend, zrecv, 0, up_z, 1), (zsend, zrecv, 1, down_z, 1),
        )
        return [
            pltpu.make_async_remote_copy(
                out.at[e, side, at], into.at[e, side, at],
                halo_s.at[e - 1, g, i], halo_r.at[e - 1, g, i], device_id=peer, device_id_type=MESH,
            )
            for out, into, side, peer, i in sides
        ]

    def send(e, t, g):
        def field(f, carry):
            for i in range(2):
                first = LEAD + i * PITCH
                last = LEAD + (ny - 2 + i) * PITCH
                ysend[e, 0, f, i] = t[f, last : last + nz].astype(BF16)
                ysend[e, 1, f, i] = t[f, first : first + nz].astype(BF16)
            high = [t[f, pl.ds(LEAD + nz - 2 + i, ny, stride=PITCH)] for i in range(2)]
            low = [t[f, pl.ds(LEAD + i, ny, stride=PITCH)] for i in range(2)]
            zsend[e, 0, f] = jnp.concatenate(high, 0).astype(BF16)
            zsend[e, 1, f] = jnp.concatenate(low, 0).astype(BF16)
            return carry

        lax.fori_loop(g * GROUP, (g + 1) * GROUP, field, 0)
        for copy in halo_copies(e, g):
            copy.start()

    def applied(e, t, f, y, plane, along_x, w):
        first = LEAD + y * PITCH
        near = plane[y + 1] + plane[y - 1]
        far = plane[y + 2] + plane[y - 2]
        near = near + (t[f, first + 1 : first + 1 + nz] + t[f, first - 1 : first - 1 + nz])
        far = far + (t[f, first + 2 : first + 2 + nz] + t[f, first - 2 : first - 2 + nz])
        unit = UNIT if e == 0 else 2.0 * UNIT
        return w[y] * plane[y] + unit * ((far + along_x[y * nz : (y + 1) * nz]) - 16.0 * near)

    def step(e, g, slot):
        at = pl.ds(g * GROUP, GROUP)
        if e:
            for i, ref in enumerate((yrecv, zrecv)):
                awaited(ref.at[e, :, at], halo_r.at[e - 1, g, i]).wait()
        t = (t0, t1, t2)[e]
        if e == 2:
            row = jnp.bitwise_and(ka + q_ref[0], nka - 1) * slots + slot
            c0, c1, c2, c3 = (coeffs[j, row] for j in range(4))
            c13 = c1 - c3

        def field(f, carry):
            for side, start in ((0, LEAD - 2), (1, LEAD + nz)):
                rows_in = zrecv[e, side, f].astype(F32)
                t[f, pl.ds(start, ny, stride=PITCH)] = rows_in[0:ny]
                t[f, pl.ds(start + 1, ny, stride=PITCH)] = rows_in[ny : 2 * ny]
            plane = {}
            for y in range(ny):
                first = LEAD + y * PITCH
                plane[y] = t[f, first : first + nz]
            whole = jnp.concatenate([plane[y] for y in range(ny)], 0)
            high = whole.astype(BF16)
            low = (whole - high.astype(F32)).astype(BF16)
            along_x = jnp.dot(
                jnp.concatenate([high, low], 1), ring[...], preferred_element_type=F32
            )
            for i in range(2):
                plane[i - 2] = yrecv[e, 0, f, i].astype(F32)
                plane[ny + i] = yrecv[e, 1, f, i].astype(F32)
            for y in range(ny):
                at = slice(LEAD + y * PITCH, LEAD + y * PITCH + nz)
                if e == 0:
                    t1[f, at] = applied(e, t, f, y, plane, along_x, w_one)
                elif e == 1:
                    t2[f, at] = applied(e, t, f, y, plane, along_x, w_two) - t0[f, at]
                else:
                    doubled = applied(e, t, f, y, plane, along_x, w_two)
                    answer = (c0 * t0[f, at] + c13 * t1[f, at]) + (c2 * plane[y] + c3 * doubled)
                    rounded = answer.astype(BF16)
                    i = f - slot * fields
                    resp[slot, i, y] = rounded
                    dacc[y] += phi[slot, i, y].astype(F32) * rounded.astype(F32)
            return carry

        lax.fori_loop(g * GROUP, (g + 1) * GROUP, field, 0)

    def groups(slot):
        per_slot = fields // GROUP
        return range(slot * per_slot, (slot + 1) * per_slot)

    def advance(slot, e):
        for g in groups(slot):
            step(e, g, slot)
            if e == 0:
                send(1, t1, g)
            elif e == 1:
                send(2, t2, g)

    for slot in range(slots):
        inner(slot)
        reduce_start(slot)
        partner_z(slot)
    for slot in range(slots):
        awaited(phi_y.at[slot], early_r.at[slot]).wait()
    for ref, i in ((pert_y, 2), (phi_z, 3), (pert_z, 4)):
        awaited(ref, early_r.at[i]).wait()
    for slot in range(slots):
        reduce_finish(slot)
        project(slot)
        advance(slot, 0)
    for e in range(1, 3):
        for slot in range(slots):
            advance(slot, e)

    lanes = nx // nka
    lane_at = lax.broadcasted_iota(jnp.int32, (nz, nx), 1)
    scale = 2.0 / (slots * nka)
    block_at = lax.shift_right_logical(lane_at, lanes.bit_length() - 1)
    blocks = [dacc[y] * scale for y in range(ny)]
    stride = nka // 2
    while stride:
        odd = jnp.bitwise_and(block_at, stride) != 0
        for i in range(nka):
            if not i & stride:
                one, two = blocks[i], blocks[i + stride]
                blocks[i] = jnp.where(odd, pltpu.roll(two, stride * lanes, 1), one)
                blocks[i + stride] = jnp.where(odd, two, pltpu.roll(one, nx - stride * lanes, 1))
        stride //= 2
    for d in range(nka):
        dsend[d] = blocks[d]
    den_copies = [
        pltpu.make_async_remote_copy(
            dsend.at[lax.rem(ka + d, nka)], drecv.at[d], den_s, den_r,
            device_id=ka_at(d), device_id_type=MESH,
        )
        for d in range(1, nka)
    ]
    for copy in den_copies:
        copy.start()
    awaited(drecv.at[1:nka], den_r).wait()
    total = dsend[ka]
    for d in range(1, nka):
        total = total + drecv[d]
    dens[...] = jnp.transpose(total)

    awaited(dsend.at[1:nka], den_s).wait()
    for slot in range(slots):
        awaited(orb.at[slot, 1:nka], first_s.at[slot]).wait()
        awaited(stage.at[slot, 1:nka], second_s.at[slot]).wait()
        awaited(red_recv.at[slot, 1:members], red_s.at[slot]).wait()
        awaited(phi_y.at[slot], early_s.at[slot]).wait()
        awaited(parts_y[slot], early_s.at[5 + slot]).wait()
        awaited(parts_z[slot], early_s.at[7 + slot]).wait()
    for ref, i in ((pert_y, 2), (phi_z, 3), (pert_z, 4)):
        awaited(ref, early_s.at[i]).wait()
    for e in range(1, 3):
        for g in range(slots * fields // GROUP):
            at = pl.ds(g * GROUP, GROUP)
            awaited(ysend.at[e, :, at], halo_s.at[e - 1, g, 0]).wait()
            awaited(zsend.at[e, :, at], halo_s.at[e - 1, g, 1]).wait()


def call(sizes, q_index, orb, coeffs, pot, pert):
    nka, nsy, nsz = sizes
    slots, fields, ny, nz, nx = orb.shape
    count = slots * fields
    groups = count // GROUP
    hbm = pl.BlockSpec(memory_space=pltpu.HBM)
    vmem = pl.BlockSpec(memory_space=pltpu.VMEM)
    dma = pltpu.SemaphoreType.DMA
    t_shape = (count, LEAD + ny * PITCH, nx)
    scratch = [
        pltpu.SMEM(coeffs.shape, F32),
        pltpu.VMEM(orb.shape, BF16),
        pltpu.VMEM(orb.shape[1:], BF16),
        pltpu.VMEM(orb.shape[1:], BF16),
        pltpu.VMEM(orb.shape, BF16),
        pltpu.VMEM(orb.shape[1:], BF16),
        pltpu.VMEM(orb.shape[1:], BF16),
        pltpu.VMEM(pot.shape, F32),
        pltpu.VMEM(pot.shape, F32),
        pltpu.VMEM(pot.shape, F32),
        pltpu.VMEM(pot.shape, F32),
        pltpu.VMEM((2 * nx, nx), BF16),
        pltpu.VMEM(t_shape, F32),
        pltpu.VMEM(t_shape, F32),
        pltpu.VMEM(t_shape, F32),
        pltpu.VMEM((40 * 8, nx), F32),
        pltpu.VMEM((nx, nx), F32),
        pltpu.VMEM((32, 8, nx), F32),
        pltpu.VMEM(pot.shape, F32),
        pltpu.VMEM((slots, 2, fields, 2, nz, nx), BF16),
        pltpu.VMEM((2, slots, fields, 2 * ny, nx), BF16),
        pltpu.VMEM((2, slots, fields, 2 * ny, nx), BF16),
        pltpu.VMEM((2, 2, nz, nx), F32),
        pltpu.VMEM((2, 2 * ny, nx), F32),
        pltpu.VMEM((2, 2 * ny, nx), F32),
        pltpu.VMEM((2, fields, 2, nz, nx), BF16),
        pltpu.VMEM((2, fields, 2, nz, nx), BF16),
        pltpu.VMEM((2, fields, 2 * ny, nx), BF16),
        pltpu.VMEM((2, fields, 2 * ny, nx), BF16),
        pltpu.VMEM((slots, 2, fields, 2 * ny, nx), BF16),
        pltpu.VMEM((8 * ny, nx), F32),
        pltpu.VMEM((3, 2, count, 2, nz, nx), BF16),
        pltpu.VMEM((3, 2, count, 2, nz, nx), BF16),
        pltpu.VMEM((3, 2, count, 2 * ny, nx), BF16),
        pltpu.VMEM((3, 2, count, 2 * ny, nx), BF16),
        pltpu.VMEM((slots, 1, nx), F32),
        pltpu.VMEM((slots, nsy * nsz, 1, nx), F32),
        pltpu.VMEM((nka, nz, nx), F32),
        pltpu.VMEM((nka, nz, nx), F32),
        dma((4,)),
        dma((slots,)),
        dma((slots,)),
        dma((slots,)),
        dma((slots,)),
        dma((slots,)),
        dma((slots,)),
        dma((9,)),
        dma((9,)),
        dma((2, groups, 2)),
        dma((2, groups, 2)),
        dma,
        dma,
    ]
    held = [pltpu.with_memory_space_constraint(x, pltpu.HBM) for x in (orb, coeffs, pot, pert)]
    return pl.pallas_call(
        functools.partial(kernel, sizes),
        out_shape=(
            pltpu.VMEM(orb.shape, BF16),
            pltpu.VMEM((nx, nz), F32),
        ),
        in_specs=[pl.BlockSpec(memory_space=pltpu.SMEM)] + [hbm] * 4,
        out_specs=(vmem, vmem),
        scratch_shapes=scratch,
        compiler_params=pltpu.CompilerParams(
            collective_id=0, has_side_effects=True, vmem_limit_bytes=48 << 20
        ),
        name="respond",
    )(q_index, *held)


def body(sizes, orbitals, coefficients, local_pot, perturb, q_index):
    orb = orbitals.reshape((orbitals.shape[0], -1) + orbitals.shape[3:])
    responses, density = call(sizes, q_index, orb, coefficients.T, local_pot, perturb)
    ny, nz, nx = local_pot.shape
    density = density.reshape((ny, nx // sizes[0], nz)).transpose(0, 2, 1)
    return responses.reshape(orbitals.shape), density


def solution(mesh):
    sizes = (mesh.shape["ka"], mesh.shape["sy"], mesh.shape["sz"])
    return jax.shard_map(
        functools.partial(body, sizes),
        mesh=mesh,
        in_specs=(
            P("ka", None, None, "sy", "sz", None),
            P(),
            P("sy", "sz", None),
            P("sy", "sz", None),
            P(),
        ),
        out_specs=(P("ka", None, None, "sy", "sz", None), P("sy", "sz", "ka")),
        check_vma=False,
    )
```

```python
import functools

import jax
import jax.numpy as jnp
from jax import lax
from jax.experimental import pallas as pl
from jax.experimental.pallas import tpu as pltpu
from jax.sharding import PartitionSpec as P

MESH = pl.DeviceIdType.MESH
F32 = jnp.float32
BF16 = jnp.bfloat16

UNIT = 0.2 * 0.5 / 12.0
EPSILON = 1e-6
BANDS = 4
GROUP = 4
PITCH = 40
LEAD = 8


def fold(value):
    return value[0:8] + value[8:16] + value[16:24] + value[24:32]


def kernel(
    sizes, q_in, orb, coeffs_in, pot, pert, resp, dens,
    q_ref, coeffs, phi, mid_a, mid_b, stage, land_a, land_b, potv, pertv, w_one, w_two, ring, t0, t1, t2, accs, entries, cf, dacc,
    phi_y, phi_z, phi_zs, pert_y, pert_z, pert_zs, part_y_a, part_y_b, part_z_a, part_z_b, part_zs, zpack,
    ysend, yrecv, zsend, zrecv, red_send, red_recv, dsend, drecv,
    load_sem, first_s, first_r, second_s, second_r, red_s, red_r, early_s, early_r, halo_s, halo_r, den_s, den_r,
):
    nka, nsy, nsz = sizes
    slots, fields, ny, nz, nx = phi.shape
    ka, sy, sz = lax.axis_index("ka"), lax.axis_index("sy"), lax.axis_index("sz")

    def ka_at(step):
        return {"ka": lax.rem(ka + step, nka)}

    def group_at(step):
        return {"sy": lax.rem(sy + step // nsz, nsy), "sz": lax.rem(sz + step % nsz, nsz)}

    members = nsy * nsz
    mids, lands = (mid_a, mid_b), (land_a, land_b)
    parts_y, parts_z = (part_y_a, part_y_b), (part_z_a, part_z_b)
    loads = [
        pltpu.make_async_copy(orb, phi, load_sem.at[0]),
        pltpu.make_async_copy(pert, pertv, load_sem.at[1]),
        pltpu.make_async_copy(pot, potv, load_sem.at[2]),
        pltpu.make_async_copy(coeffs_in, coeffs, load_sem.at[3]),
        pltpu.make_async_copy(q_in, q_ref, load_sem.at[4]),
    ]
    for copy in loads:
        copy.start()

    barrier = pltpu.get_barrier_semaphore()
    peers = [ka_at(d) for d in range(1, nka)] + [group_at(d) for d in range(1, members)]
    for peer in peers:
        pl.semaphore_signal(barrier, inc=1, device_id=peer, device_id_type=MESH)
    pl.semaphore_wait(barrier, len(peers))

    up_y = {"sy": lax.rem(sy + 1, nsy)}
    down_y = {"sy": lax.rem(sy + nsy - 1, nsy)}
    up_z = {"sz": lax.rem(sz + 1, nsz)}
    down_z = {"sz": lax.rem(sz + nsz - 1, nsz)}

    def early(i, high, low, into, peers):
        for src, side, peer in ((high, 0, peers[0]), (low, 1, peers[1])):
            pltpu.make_async_remote_copy(
                src, into.at[side], early_s.at[i], early_r.at[i], device_id=peer, device_id_type=MESH
            ).start()

    along_y, along_z = (up_y, down_y), (up_z, down_z)

    def pack_z(read):
        zpack[...] = read(slice(nz - 8, nz)).astype(F32).reshape(8 * ny, nx)
        high = [zpack[pl.ds(6 + i, ny, stride=8)] for i in range(2)]
        zpack[...] = read(slice(0, 8)).astype(F32).reshape(8 * ny, nx)
        low = [zpack[pl.ds(i, ny, stride=8)] for i in range(2)]
        return jnp.concatenate(high, 0), jnp.concatenate(low, 0)

    def awaited(ref, sem):
        return pltpu.make_async_copy(ref, ref, sem)

    def routed(src, dst, send, recv):
        return [
            pltpu.make_async_remote_copy(
                src.at[d], dst.at[d], send, recv, device_id=ka_at(d), device_id_type=MESH
            )
            for d in range(1, nka)
        ]

    def piece(of):
        return jnp.bitwise_and(-q_ref[0] - of, nka - 1)

    for slot in range(slots):
        for copy in routed(orb.at[slot], mids[slot], first_s.at[slot], first_r.at[slot]):
            copy.start()

    for slot in range(slots):
        early(slot, orb.at[slot, :, ny - 2 : ny], orb.at[slot, :, 0:2], phi_y.at[slot], along_y)
    early(2, pert.at[ny - 2 : ny], pert.at[0:2], pert_y, along_y)
    for copy in loads:
        copy.wait()
    for slot in range(slots):

        def own_field(i, carry):
            high, low = pack_z(lambda at: phi[slot, i, :, at])
            phi_zs[0, slot, i] = high.astype(BF16)
            phi_zs[1, slot, i] = low.astype(BF16)
            return carry

        lax.fori_loop(0, fields, own_field, 0)
    pert_zs[0], pert_zs[1] = pack_z(lambda at: pertv[:, at])
    early(3, phi_zs.at[0], phi_zs.at[1], phi_z, along_z)
    early(4, pert_zs.at[0], pert_zs.at[1], pert_z, along_z)
    w_one[...] = 0.2 * potv[...] - 0.25
    w_two[...] = 0.4 * potv[...] - 0.5
    dacc[...] = jnp.zeros_like(dacc)

    row_at = lax.broadcasted_iota(jnp.int32, (nx, nx), 0)
    column_at = lax.broadcasted_iota(jnp.int32, (nx, nx), 1)
    apart = jnp.bitwise_and(row_at - column_at, nx - 1)
    circle = jnp.where(
        (apart == 1) | (apart == nx - 1), -16.0, jnp.where((apart == 2) | (apart == nx - 2), 1.0, 0.0)
    ).astype(BF16)
    ring[0:nx] = circle
    ring[nx : 2 * nx] = circle
    ones = jnp.ones((8, nx), BF16)
    entries[...] = jnp.zeros_like(entries)

    for slot in range(slots):
        mid, land = mids[slot], lands[slot]
        mid[0] = phi[slot, 0]
        awaited(mid.at[1:nka], first_r.at[slot]).wait()
        land[0] = mid[piece(0)]
        for d in range(1, nka):
            stage[slot, d] = mid[piece(d)]
        for copy in routed(stage.at[slot], land, second_s.at[slot], second_r.at[slot]):
            copy.start()

    def inner(slot):
        accs[...] = jnp.zeros_like(accs)

        def plane(y, carry):
            pe = pertv[y]
            source = [
                (pe * phi[slot, 2 * c, y].astype(F32), pe * phi[slot, 2 * c + 1, y].astype(F32))
                for c in range(BANDS)
            ]
            for b in range(BANDS):
                p_re = lands[slot][piece(2 * b), y].astype(F32)
                p_im = lands[slot][piece(2 * b + 1), y].astype(F32)
                at = 8 * (32 + b)
                accs[at : at + 8] += fold(p_re * p_re + p_im * p_im)
                for c in range(BANDS):
                    s_re, s_im = source[c]
                    at = 8 * (b * BANDS + c)
                    accs[at : at + 8] += fold(p_re * s_re + p_im * s_im)
                    at += 8 * 16
                    accs[at : at + 8] += fold(p_re * s_im - p_im * s_re)
            return carry

        awaited(lands[slot].at[1:nka], second_r.at[slot]).wait()
        lax.fori_loop(0, ny, plane, 0)

    def reduce_start(slot):
        count = 32 + BANDS
        summed = accs[pl.ds(0, count, stride=8)]
        for i in range(1, 8):
            summed = summed + accs[pl.ds(i, count, stride=8)]
        entries[0:32] = summed[0:32]
        for b in range(BANDS):
            norm = jnp.broadcast_to(summed[32 + b : 33 + b], (BANDS, nx))
            entries[64 + b * BANDS : 64 + (b + 1) * BANDS] = norm
            entries[80 + b * BANDS : 80 + (b + 1) * BANDS] = norm
        whole = entries[...]
        row = jnp.zeros((8, nx), F32)
        for _ in range(3):
            rounded = whole.astype(BF16)
            row = row + lax.dot_general(
                ones, rounded, (((1,), (1,)), ((), ())), preferred_element_type=F32
            )
            whole = whole - rounded.astype(F32)
        red_send[slot] = row[0:1]
        for d in range(1, members):
            pltpu.make_async_remote_copy(
                red_send.at[slot], red_recv.at[slot, d], red_s.at[slot], red_r.at[slot],
                device_id=group_at(d), device_id_type=MESH,
            ).start()

    def reduce_finish(slot):
        awaited(red_recv.at[slot, 1:members], red_r.at[slot]).wait()
        total = red_send[slot]
        for d in range(1, members):
            total = total + red_recv[slot, d]
        coef = total / (pltpu.roll(total, 64, 1) + EPSILON)
        for i in range(32):
            cf[i] = jnp.broadcast_to(coef[:, i : i + 1], (8, nx))

    def partner_halo(slot):
        land = lands[slot]
        early(5 + slot, land.at[:, ny - 2 : ny], land.at[:, 0:2], parts_y[slot], along_y)

        def field(i, carry):
            high, low = pack_z(lambda at: lands[slot][i, :, at])
            part_zs[slot, 0, i] = high.astype(BF16)
            part_zs[slot, 1, i] = low.astype(BF16)
            return carry

        lax.fori_loop(0, fields, field, 0)
        early(7 + slot, part_zs.at[slot, 0], part_zs.at[slot, 1], parts_z[slot], along_z)

    def projected(pe, own, partner):
        def tiles(value):
            return value.astype(F32).reshape(2, 8, nx)

        pe = tiles(pe)
        partner = [tiles(value) for value in partner]
        out = []
        for c in range(BANDS):
            out_re = pe * tiles(own[2 * c])
            out_im = pe * tiles(own[2 * c + 1])
            for b in range(BANDS):
                c_re = cf[b * BANDS + c]
                c_im = cf[16 + b * BANDS + c]
                p_re, p_im = partner[2 * b], partner[2 * b + 1]
                out_re = out_re - (c_re * p_re - c_im * p_im)
                out_im = out_im - (c_im * p_re + c_re * p_im)
            out += [out_re.reshape(16, nx), out_im.reshape(16, nx)]
        return out

    def project(slot):
        every = range(fields)
        land, part_y, part_z = lands[slot], parts_y[slot], parts_z[slot]
        first_field = slot * fields

        def plane(y, carry):
            for half in range(nz // 16):
                at = pl.ds(16 * half, 16)
                row = pl.ds(pl.multiple_of(LEAD + y * PITCH + 16 * half, 8), 16)
                out = projected(
                    pertv[y, at],
                    [phi[slot, i, y, at] for i in every],
                    [land[piece(i), y, at] for i in every],
                )
                for i in every:
                    t0[first_field + i, row] = out[i]
            return carry

        lax.fori_loop(0, ny, plane, 0)

        def outer_plane(i, carry):
            side, layer = lax.shift_right_logical(i, 1), jnp.bitwise_and(i, 1)
            for half in range(nz // 16):
                at = pl.ds(16 * half, 16)
                out = projected(
                    pert_y[side, layer, at],
                    [phi_y[slot, side, f, layer, at] for f in every],
                    [part_y[side, piece(f), layer, at] for f in every],
                )
                for f in every:
                    yrecv[0, side, first_field + f, layer, at] = out[f].astype(BF16)
            return carry

        def outer_rows(side, carry):
            out = projected(
                pert_z[side],
                [phi_z[side, slot, f] for f in every],
                [part_z[side, piece(f)] for f in every],
            )
            for f in every:
                zrecv[0, side, first_field + f] = out[f].astype(BF16)
            return carry

        awaited(part_y, early_r.at[5 + slot]).wait()
        awaited(part_z, early_r.at[7 + slot]).wait()
        lax.fori_loop(0, 4, outer_plane, 0)
        lax.fori_loop(0, 2, outer_rows, 0)

    def halo_copies(e, g):
        at = pl.ds(g * GROUP, GROUP)
        sides = (
            (ysend, yrecv, 0, up_y, 0), (ysend, yrecv, 1, down_y, 0),
            (zsend, zrecv, 0, up_z, 1), (zsend, zrecv, 1, down_z, 1),
        )
        return [
            pltpu.make_async_remote_copy(
                out.at[e, side, at], into.at[e, side, at],
                halo_s.at[e - 1, g, i], halo_r.at[e - 1, g, i], device_id=peer, device_id_type=MESH,
            )
            for out, into, side, peer, i in sides
        ]

    def send(e, t, g):
        def field(f, carry):
            for i in range(2):
                first = LEAD + i * PITCH
                last = LEAD + (ny - 2 + i) * PITCH
                ysend[e, 0, f, i] = t[f, last : last + nz].astype(BF16)
                ysend[e, 1, f, i] = t[f, first : first + nz].astype(BF16)
            high = [t[f, pl.ds(LEAD + nz - 2 + i, ny, stride=PITCH)] for i in range(2)]
            low = [t[f, pl.ds(LEAD + i, ny, stride=PITCH)] for i in range(2)]
            zsend[e, 0, f] = jnp.concatenate(high, 0).astype(BF16)
            zsend[e, 1, f] = jnp.concatenate(low, 0).astype(BF16)
            return carry

        lax.fori_loop(g * GROUP, (g + 1) * GROUP, field, 0, unroll=2)
        for copy in halo_copies(e, g):
            copy.start()

    def applied(e, t, f, y, plane, along_x, w):
        first = LEAD + y * PITCH
        near = plane[y + 1] + plane[y - 1]
        far = plane[y + 2] + plane[y - 2]
        near = near + (t[f, first + 1 : first + 1 + nz] + t[f, first - 1 : first - 1 + nz])
        far = far + (t[f, first + 2 : first + 2 + nz] + t[f, first - 2 : first - 2 + nz])
        unit = UNIT if e == 0 else 2.0 * UNIT
        return w[y] * plane[y] + unit * ((far + along_x[y * nz : (y + 1) * nz]) - 16.0 * near)

    def step(e, g, slot):
        at = pl.ds(g * GROUP, GROUP)
        if e:
            for i, ref in enumerate((yrecv, zrecv)):
                awaited(ref.at[e, :, at], halo_r.at[e - 1, g, i]).wait()
        t = (t0, t1, t2)[e]
        if e == 2:
            row = jnp.bitwise_and(ka + q_ref[0], nka - 1) * slots + slot
            c0, c1, c2, c3 = (coeffs[j, row] for j in range(4))
            c13 = c1 - c3

        def field(f, carry):
            for side, start in ((0, LEAD - 2), (1, LEAD + nz)):
                rows_in = zrecv[e, side, f].astype(F32)
                t[f, pl.ds(start, ny, stride=PITCH)] = rows_in[0:ny]
                t[f, pl.ds(start + 1, ny, stride=PITCH)] = rows_in[ny : 2 * ny]
            plane = {}
            for y in range(ny):
                first = LEAD + y * PITCH
                plane[y] = t[f, first : first + nz]
            whole = jnp.concatenate([plane[y] for y in range(ny)], 0)
            high = whole.astype(BF16)
            low = (whole - high.astype(F32)).astype(BF16)
            along_x = jnp.dot(
                jnp.concatenate([high, low], 1), ring[...], preferred_element_type=F32
            )
            for i in range(2):
                plane[i - 2] = yrecv[e, 0, f, i].astype(F32)
                plane[ny + i] = yrecv[e, 1, f, i].astype(F32)
            for y in range(ny):
                at = slice(LEAD + y * PITCH, LEAD + y * PITCH + nz)
                if e == 0:
                    t1[f, at] = applied(e, t, f, y, plane, along_x, w_one)
                elif e == 1:
                    t2[f, at] = applied(e, t, f, y, plane, along_x, w_two) - t0[f, at]
                else:
                    doubled = applied(e, t, f, y, plane, along_x, w_two)
                    answer = (c0 * t0[f, at] + c13 * t1[f, at]) + (c2 * plane[y] + c3 * doubled)
                    rounded = answer.astype(BF16)
                    i = f - slot * fields
                    resp[slot, i, y] = rounded
                    dacc[y] += phi[slot, i, y].astype(F32) * rounded.astype(F32)
            return carry

        lax.fori_loop(g * GROUP, (g + 1) * GROUP, field, 0, unroll=2)

    def groups(slot):
        per_slot = fields // GROUP
        return range(slot * per_slot, (slot + 1) * per_slot)

    def advance(slot, e):
        for g in groups(slot):
            step(e, g, slot)
            if e == 0:
                send(1, t1, g)
            elif e == 1:
                send(2, t2, g)

    for slot in range(slots):
        inner(slot)
        reduce_start(slot)
        partner_halo(slot)
    for slot in range(slots):
        awaited(phi_y.at[slot], early_r.at[slot]).wait()
    for ref, i in ((pert_y, 2), (phi_z, 3), (pert_z, 4)):
        awaited(ref, early_r.at[i]).wait()
    for slot in range(slots):
        reduce_finish(slot)
        project(slot)
        advance(slot, 0)
    for e in range(1, 3):
        for slot in range(slots):
            advance(slot, e)

    lanes = nx // nka
    lane_at = lax.broadcasted_iota(jnp.int32, (nz, nx), 1)
    scale = 2.0 / (slots * nka)
    block_at = lax.shift_right_logical(lane_at, lanes.bit_length() - 1)
    blocks = [dacc[y] * scale for y in range(ny)]
    stride = nka // 2
    while stride:
        odd = jnp.bitwise_and(block_at, stride) != 0
        for i in range(nka):
            if not i & stride:
                one, two = blocks[i], blocks[i + stride]
                blocks[i] = jnp.where(odd, pltpu.roll(two, stride * lanes, 1), one)
                blocks[i + stride] = jnp.where(odd, two, pltpu.roll(one, nx - stride * lanes, 1))
        stride //= 2
    for d in range(nka):
        dsend[d] = blocks[d]
    den_copies = [
        pltpu.make_async_remote_copy(
            dsend.at[lax.rem(ka + d, nka)], drecv.at[d], den_s, den_r,
            device_id=ka_at(d), device_id_type=MESH,
        )
        for d in range(1, nka)
    ]
    for copy in den_copies:
        copy.start()
    awaited(drecv.at[1:nka], den_r).wait()
    total = dsend[ka]
    for d in range(1, nka):
        total = total + drecv[d]
    dens[...] = jnp.transpose(total)

    awaited(dsend.at[1:nka], den_s).wait()
    for slot in range(slots):
        awaited(orb.at[slot, 1:nka], first_s.at[slot]).wait()
        awaited(stage.at[slot, 1:nka], second_s.at[slot]).wait()
        awaited(red_recv.at[slot, 1:members], red_s.at[slot]).wait()
        awaited(phi_y.at[slot], early_s.at[slot]).wait()
        awaited(parts_y[slot], early_s.at[5 + slot]).wait()
        awaited(parts_z[slot], early_s.at[7 + slot]).wait()
    for ref, i in ((pert_y, 2), (phi_z, 3), (pert_z, 4)):
        awaited(ref, early_s.at[i]).wait()
    for e in range(1, 3):
        for g in range(slots * fields // GROUP):
            at = pl.ds(g * GROUP, GROUP)
            awaited(ysend.at[e, :, at], halo_s.at[e - 1, g, 0]).wait()
            awaited(zsend.at[e, :, at], halo_s.at[e - 1, g, 1]).wait()


def call(sizes, q_index, orb, coeffs, pot, pert):
    nka, nsy, nsz = sizes
    slots, fields, ny, nz, nx = orb.shape
    count = slots * fields
    groups = count // GROUP
    hbm = pl.BlockSpec(memory_space=pltpu.HBM)
    vmem = pl.BlockSpec(memory_space=pltpu.VMEM)
    dma = pltpu.SemaphoreType.DMA
    t_shape = (count, LEAD + ny * PITCH, nx)
    scratch = [
        pltpu.SMEM(q_index.shape, jnp.int32),
        pltpu.SMEM(coeffs.shape, F32),
        pltpu.VMEM(orb.shape, BF16),
        pltpu.VMEM(orb.shape[1:], BF16),
        pltpu.VMEM(orb.shape[1:], BF16),
        pltpu.VMEM(orb.shape, BF16),
        pltpu.VMEM(orb.shape[1:], BF16),
        pltpu.VMEM(orb.shape[1:], BF16),
        pltpu.VMEM(pot.shape, F32),
        pltpu.VMEM(pot.shape, F32),
        pltpu.VMEM(pot.shape, F32),
        pltpu.VMEM(pot.shape, F32),
        pltpu.VMEM((2 * nx, nx), BF16),
        pltpu.VMEM(t_shape, F32),
        pltpu.VMEM(t_shape, F32),
        pltpu.VMEM(t_shape, F32),
        pltpu.VMEM((40 * 8, nx), F32),
        pltpu.VMEM((nx, nx), F32),
        pltpu.VMEM((32, 8, nx), F32),
        pltpu.VMEM(pot.shape, F32),
        pltpu.VMEM((slots, 2, fields, 2, nz, nx), BF16),
        pltpu.VMEM((2, slots, fields, 2 * ny, nx), BF16),
        pltpu.VMEM((2, slots, fields, 2 * ny, nx), BF16),
        pltpu.VMEM((2, 2, nz, nx), F32),
        pltpu.VMEM((2, 2 * ny, nx), F32),
        pltpu.VMEM((2, 2 * ny, nx), F32),
        pltpu.VMEM((2, fields, 2, nz, nx), BF16),
        pltpu.VMEM((2, fields, 2, nz, nx), BF16),
        pltpu.VMEM((2, fields, 2 * ny, nx), BF16),
        pltpu.VMEM((2, fields, 2 * ny, nx), BF16),
        pltpu.VMEM((slots, 2, fields, 2 * ny, nx), BF16),
        pltpu.VMEM((8 * ny, nx), F32),
        pltpu.VMEM((3, 2, count, 2, nz, nx), BF16),
        pltpu.VMEM((3, 2, count, 2, nz, nx), BF16),
        pltpu.VMEM((3, 2, count, 2 * ny, nx), BF16),
        pltpu.VMEM((3, 2, count, 2 * ny, nx), BF16),
        pltpu.VMEM((slots, 1, nx), F32),
        pltpu.VMEM((slots, nsy * nsz, 1, nx), F32),
        pltpu.VMEM((nka, nz, nx), F32),
        pltpu.VMEM((nka, nz, nx), F32),
        dma((5,)),
        dma((slots,)),
        dma((slots,)),
        dma((slots,)),
        dma((slots,)),
        dma((slots,)),
        dma((slots,)),
        dma((9,)),
        dma((9,)),
        dma((2, groups, 2)),
        dma((2, groups, 2)),
        dma,
        dma,
    ]
    held = [pltpu.with_memory_space_constraint(x, pltpu.HBM) for x in (orb, coeffs, pot, pert)]
    return pl.pallas_call(
        functools.partial(kernel, sizes),
        out_shape=(
            pltpu.VMEM(orb.shape, BF16),
            pltpu.VMEM((nx, nz), F32),
        ),
        in_specs=[pl.BlockSpec(memory_space=pl.ANY)] + [hbm] * 4,
        out_specs=(vmem, vmem),
        scratch_shapes=scratch,
        compiler_params=pltpu.CompilerParams(
            collective_id=0, has_side_effects=True, vmem_limit_bytes=48 << 20
        ),
        name="respond",
    )(q_index, *held)


def body(sizes, orbitals, coefficients, local_pot, perturb, q_index):
    orb = orbitals.reshape((orbitals.shape[0], -1) + orbitals.shape[3:])
    responses, density = call(sizes, q_index, orb, coefficients.T, local_pot, perturb)
    ny, nz, nx = local_pot.shape
    density = density.reshape((ny, nx // sizes[0], nz)).transpose(0, 2, 1)
    return responses.reshape(orbitals.shape), density


def solution(mesh):
    sizes = (mesh.shape["ka"], mesh.shape["sy"], mesh.shape["sz"])
    return jax.shard_map(
        functools.partial(body, sizes),
        mesh=mesh,
        in_specs=(
            P("ka", None, None, "sy", "sz", None),
            P(),
            P("sy", "sz", None),
            P("sy", "sz", None),
            P(),
        ),
        out_specs=(P("ka", None, None, "sy", "sz", None), P("sy", "sz", "ka")),
        check_vma=False,
    )
```

```python
import functools

import jax
import jax.numpy as jnp
from jax import lax
from jax.experimental import pallas as pl
from jax.experimental.pallas import tpu as pltpu
from jax.sharding import PartitionSpec as P

MESH = pl.DeviceIdType.MESH
F32 = jnp.float32
BF16 = jnp.bfloat16

UNIT = 0.2 * 0.5 / 12.0
EPSILON = 1e-6
BANDS = 4
GROUP = 4
PITCH = 40
LEAD = 8


def fold(value):
    return value[0:8] + value[8:16] + value[16:24] + value[24:32]


def kernel(
    shift, sizes, q_in, orb, coeffs_in, pot, pert, resp, dens,
    q_ref, coeffs, phi, mid_a, mid_b, stage, land_a, land_b, potv, pertv, w_one, w_two, ring, t0, t1, t2, accs, entries, cf, dacc,
    phi_y, phi_z, phi_zs, pert_y, pert_z, pert_zs, part_y_a, part_y_b, part_z_a, part_z_b, part_zs, zpack,
    ysend, yrecv, zsend, zrecv, red_send, red_recv, dsend, drecv,
    load_sem, first_s, first_r, route_s, route_r, red_s, red_r, early_s, early_r, halo_s, halo_r, den_s, den_r,
):
    nka, nsy, nsz = sizes
    slots, fields, ny, nz, nx = phi.shape
    ka, sy, sz = lax.axis_index("ka"), lax.axis_index("sy"), lax.axis_index("sz")

    def ka_at(step):
        return {"ka": lax.rem(ka + step, nka)}

    def group_at(step):
        return {"sy": lax.rem(sy + step // nsz, nsy), "sz": lax.rem(sz + step % nsz, nsz)}

    members = nsy * nsz
    mids, lands = (mid_a, mid_b), (land_a, land_b)
    direct = shift is not None
    parts_y, parts_z = (part_y_a, part_y_b), (part_z_a, part_z_b)
    loads = [
        pltpu.make_async_copy(orb, phi, load_sem.at[0]),
        pltpu.make_async_copy(pert, pertv, load_sem.at[1]),
        pltpu.make_async_copy(pot, potv, load_sem.at[2]),
        pltpu.make_async_copy(coeffs_in, coeffs, load_sem.at[3]),
        pltpu.make_async_copy(q_in, q_ref, load_sem.at[4]),
    ]
    for copy in loads:
        copy.start()

    barrier = pltpu.get_barrier_semaphore()
    peers = [ka_at(d) for d in range(1, nka)] + [group_at(d) for d in range(1, members)]
    for peer in peers:
        pl.semaphore_signal(barrier, inc=1, device_id=peer, device_id_type=MESH)
    pl.semaphore_wait(barrier, len(peers))

    up_y = {"sy": lax.rem(sy + 1, nsy)}
    down_y = {"sy": lax.rem(sy + nsy - 1, nsy)}
    up_z = {"sz": lax.rem(sz + 1, nsz)}
    down_z = {"sz": lax.rem(sz + nsz - 1, nsz)}

    def early(i, high, low, into, peers):
        for src, side, peer in ((high, 0, peers[0]), (low, 1, peers[1])):
            pltpu.make_async_remote_copy(
                src, into.at[side], early_s.at[i], early_r.at[i], device_id=peer, device_id_type=MESH
            ).start()

    along_y, along_z = (up_y, down_y), (up_z, down_z)

    def pack_z(read):
        zpack[...] = read(slice(nz - 8, nz)).astype(F32).reshape(8 * ny, nx)
        high = [zpack[pl.ds(6 + i, ny, stride=8)] for i in range(2)]
        zpack[...] = read(slice(0, 8)).astype(F32).reshape(8 * ny, nx)
        low = [zpack[pl.ds(i, ny, stride=8)] for i in range(2)]
        return jnp.concatenate(high, 0), jnp.concatenate(low, 0)

    def awaited(ref, sem):
        return pltpu.make_async_copy(ref, ref, sem)

    def piece(of):
        return of if direct else jnp.bitwise_and(-q_ref[0] - of, nka - 1)

    def routed(src, dst, send, recv):
        for d in range(1, nka):
            pltpu.make_async_remote_copy(
                src.at[d], dst.at[d], send, recv, device_id=ka_at(d), device_id_type=MESH
            ).start()

    for slot in range(slots):
        if not direct:
            routed(orb.at[slot], mids[slot], first_s.at[slot], first_r.at[slot])
        elif shift:
            pltpu.make_async_remote_copy(
                orb.at[slot], lands[slot], route_s.at[slot], route_r.at[slot],
                device_id=ka_at(nka - shift), device_id_type=MESH,
            ).start()
        else:
            pltpu.make_async_copy(orb.at[slot], lands[slot], route_r.at[slot]).start()

    for slot in range(slots):
        early(slot, orb.at[slot, :, ny - 2 : ny], orb.at[slot, :, 0:2], phi_y.at[slot], along_y)
    early(2, pert.at[ny - 2 : ny], pert.at[0:2], pert_y, along_y)
    for copy in loads:
        copy.wait()
    for slot in range(slots):

        def own_field(i, carry):
            high, low = pack_z(lambda at: phi[slot, i, :, at])
            phi_zs[0, slot, i] = high.astype(BF16)
            phi_zs[1, slot, i] = low.astype(BF16)
            return carry

        lax.fori_loop(0, fields, own_field, 0)
    pert_zs[0], pert_zs[1] = pack_z(lambda at: pertv[:, at])
    early(3, phi_zs.at[0], phi_zs.at[1], phi_z, along_z)
    early(4, pert_zs.at[0], pert_zs.at[1], pert_z, along_z)
    w_one[...] = 0.2 * potv[...] - 0.25
    w_two[...] = 0.4 * potv[...] - 0.5
    dacc[...] = jnp.zeros_like(dacc)

    row_at = lax.broadcasted_iota(jnp.int32, (nx, nx), 0)
    column_at = lax.broadcasted_iota(jnp.int32, (nx, nx), 1)
    apart = jnp.bitwise_and(row_at - column_at, nx - 1)
    circle = jnp.where(
        (apart == 1) | (apart == nx - 1), -16.0, jnp.where((apart == 2) | (apart == nx - 2), 1.0, 0.0)
    ).astype(BF16)
    ring[0:nx] = circle
    ring[nx : 2 * nx] = circle
    ones = jnp.ones((8, nx), BF16)
    entries[...] = jnp.zeros_like(entries)

    if not direct:
        for slot in range(slots):
            mid, land = mids[slot], lands[slot]
            mid[0] = phi[slot, 0]
            awaited(mid.at[1:nka], first_r.at[slot]).wait()
            land[0] = mid[piece(0)]
            for d in range(1, nka):
                stage[slot, d] = mid[piece(d)]
            routed(stage.at[slot], land, route_s.at[slot], route_r.at[slot])

    def inner(slot):
        accs[...] = jnp.zeros_like(accs)

        def plane(y, carry):
            pe = pertv[y]
            source = [
                (pe * phi[slot, 2 * c, y].astype(F32), pe * phi[slot, 2 * c + 1, y].astype(F32))
                for c in range(BANDS)
            ]
            for b in range(BANDS):
                p_re = lands[slot][piece(2 * b), y].astype(F32)
                p_im = lands[slot][piece(2 * b + 1), y].astype(F32)
                at = 8 * (32 + b)
                accs[at : at + 8] += fold(p_re * p_re + p_im * p_im)
                for c in range(BANDS):
                    s_re, s_im = source[c]
                    at = 8 * (b * BANDS + c)
                    accs[at : at + 8] += fold(p_re * s_re + p_im * s_im)
                    at += 8 * 16
                    accs[at : at + 8] += fold(p_re * s_im - p_im * s_re)
            return carry

        landed = lands[slot] if direct else lands[slot].at[1:nka]
        awaited(landed, route_r.at[slot]).wait()
        lax.fori_loop(0, ny, plane, 0)

    def reduce_start(slot):
        count = 32 + BANDS
        summed = accs[pl.ds(0, count, stride=8)]
        for i in range(1, 8):
            summed = summed + accs[pl.ds(i, count, stride=8)]
        entries[0:32] = summed[0:32]
        for b in range(BANDS):
            norm = jnp.broadcast_to(summed[32 + b : 33 + b], (BANDS, nx))
            entries[64 + b * BANDS : 64 + (b + 1) * BANDS] = norm
            entries[80 + b * BANDS : 80 + (b + 1) * BANDS] = norm
        whole = entries[...]
        row = jnp.zeros((8, nx), F32)
        for _ in range(3):
            rounded = whole.astype(BF16)
            row = row + lax.dot_general(
                ones, rounded, (((1,), (1,)), ((), ())), preferred_element_type=F32
            )
            whole = whole - rounded.astype(F32)
        red_send[slot] = row[0:1]
        for d in range(1, members):
            pltpu.make_async_remote_copy(
                red_send.at[slot], red_recv.at[slot, d], red_s.at[slot], red_r.at[slot],
                device_id=group_at(d), device_id_type=MESH,
            ).start()

    def reduce_finish(slot):
        awaited(red_recv.at[slot, 1:members], red_r.at[slot]).wait()
        total = red_send[slot]
        for d in range(1, members):
            total = total + red_recv[slot, d]
        coef = total / (pltpu.roll(total, 64, 1) + EPSILON)
        for i in range(32):
            cf[i] = jnp.broadcast_to(coef[:, i : i + 1], (8, nx))

    def partner_halo(slot):
        land = lands[slot]
        early(5 + slot, land.at[:, ny - 2 : ny], land.at[:, 0:2], parts_y[slot], along_y)

        def field(i, carry):
            high, low = pack_z(lambda at: lands[slot][i, :, at])
            part_zs[slot, 0, i] = high.astype(BF16)
            part_zs[slot, 1, i] = low.astype(BF16)
            return carry

        lax.fori_loop(0, fields, field, 0)
        early(7 + slot, part_zs.at[slot, 0], part_zs.at[slot, 1], parts_z[slot], along_z)

    def projected(pe, own, partner):
        def tiles(value):
            return value.astype(F32).reshape(2, 8, nx)

        pe = tiles(pe)
        partner = [tiles(value) for value in partner]
        out = []
        for c in range(BANDS):
            out_re = pe * tiles(own[2 * c])
            out_im = pe * tiles(own[2 * c + 1])
            for b in range(BANDS):
                c_re = cf[b * BANDS + c]
                c_im = cf[16 + b * BANDS + c]
                p_re, p_im = partner[2 * b], partner[2 * b + 1]
                out_re = out_re - (c_re * p_re - c_im * p_im)
                out_im = out_im - (c_im * p_re + c_re * p_im)
            out += [out_re.reshape(16, nx), out_im.reshape(16, nx)]
        return out

    def project(slot):
        every = range(fields)
        land, part_y, part_z = lands[slot], parts_y[slot], parts_z[slot]
        first_field = slot * fields

        def plane(y, carry):
            for half in range(nz // 16):
                at = pl.ds(16 * half, 16)
                row = pl.ds(pl.multiple_of(LEAD + y * PITCH + 16 * half, 8), 16)
                out = projected(
                    pertv[y, at],
                    [phi[slot, i, y, at] for i in every],
                    [land[piece(i), y, at] for i in every],
                )
                for i in every:
                    t0[first_field + i, row] = out[i]
            return carry

        lax.fori_loop(0, ny, plane, 0)

        def outer_plane(i, carry):
            side, layer = lax.shift_right_logical(i, 1), jnp.bitwise_and(i, 1)
            for half in range(nz // 16):
                at = pl.ds(16 * half, 16)
                out = projected(
                    pert_y[side, layer, at],
                    [phi_y[slot, side, f, layer, at] for f in every],
                    [part_y[side, piece(f), layer, at] for f in every],
                )
                for f in every:
                    yrecv[0, side, first_field + f, layer, at] = out[f].astype(BF16)
            return carry

        def outer_rows(side, carry):
            out = projected(
                pert_z[side],
                [phi_z[side, slot, f] for f in every],
                [part_z[side, piece(f)] for f in every],
            )
            for f in every:
                zrecv[0, side, first_field + f] = out[f].astype(BF16)
            return carry

        awaited(part_y, early_r.at[5 + slot]).wait()
        awaited(part_z, early_r.at[7 + slot]).wait()
        lax.fori_loop(0, 4, outer_plane, 0)
        lax.fori_loop(0, 2, outer_rows, 0)

    def each(g, field):
        def pair(i, carry):
            for j in range(2):
                field(g * GROUP + 2 * i + j, 0)
            return carry

        lax.fori_loop(0, GROUP // 2, pair, 0)

    def halo_copies(e, g):
        at = pl.ds(g * GROUP, GROUP)
        sides = (
            (ysend, yrecv, 0, up_y, 0), (ysend, yrecv, 1, down_y, 0),
            (zsend, zrecv, 0, up_z, 1), (zsend, zrecv, 1, down_z, 1),
        )
        return [
            pltpu.make_async_remote_copy(
                out.at[e, side, at], into.at[e, side, at],
                halo_s.at[e - 1, g, i], halo_r.at[e - 1, g, i], device_id=peer, device_id_type=MESH,
            )
            for out, into, side, peer, i in sides
        ]

    def send(e, t, g):
        def field(f, carry):
            for i in range(2):
                first = LEAD + i * PITCH
                last = LEAD + (ny - 2 + i) * PITCH
                ysend[e, 0, f, i] = t[f, last : last + nz].astype(BF16)
                ysend[e, 1, f, i] = t[f, first : first + nz].astype(BF16)
            high = [t[f, pl.ds(LEAD + nz - 2 + i, ny, stride=PITCH)] for i in range(2)]
            low = [t[f, pl.ds(LEAD + i, ny, stride=PITCH)] for i in range(2)]
            zsend[e, 0, f] = jnp.concatenate(high, 0).astype(BF16)
            zsend[e, 1, f] = jnp.concatenate(low, 0).astype(BF16)
            return carry

        each(g, field)
        for copy in halo_copies(e, g):
            copy.start()

    def applied(e, t, f, y, plane, along_x, w):
        first = LEAD + y * PITCH
        near = plane[y + 1] + plane[y - 1]
        far = plane[y + 2] + plane[y - 2]
        near = near + (t[f, first + 1 : first + 1 + nz] + t[f, first - 1 : first - 1 + nz])
        far = far + (t[f, first + 2 : first + 2 + nz] + t[f, first - 2 : first - 2 + nz])
        unit = UNIT if e == 0 else 2.0 * UNIT
        return w[y] * plane[y] + unit * ((far + along_x[y * nz : (y + 1) * nz]) - 16.0 * near)

    def step(e, g, slot):
        at = pl.ds(g * GROUP, GROUP)
        if e:
            for i, ref in enumerate((yrecv, zrecv)):
                awaited(ref.at[e, :, at], halo_r.at[e - 1, g, i]).wait()
        t = (t0, t1, t2)[e]
        if e == 2:
            row = jnp.bitwise_and(ka + (shift if direct else q_ref[0]), nka - 1) * slots + slot
            c0, c1, c2, c3 = (coeffs[j, row] for j in range(4))
            c13 = c1 - c3

        def field(f, carry):
            for side, start in ((0, LEAD - 2), (1, LEAD + nz)):
                rows_in = zrecv[e, side, f].astype(F32)
                t[f, pl.ds(start, ny, stride=PITCH)] = rows_in[0:ny]
                t[f, pl.ds(start + 1, ny, stride=PITCH)] = rows_in[ny : 2 * ny]
            plane = {}
            for y in range(ny):
                first = LEAD + y * PITCH
                plane[y] = t[f, first : first + nz]
            whole = jnp.concatenate([plane[y] for y in range(ny)], 0)
            high = whole.astype(BF16)
            low = (whole - high.astype(F32)).astype(BF16)
            along_x = jnp.dot(
                jnp.concatenate([high, low], 1), ring[...], preferred_element_type=F32
            )
            for i in range(2):
                plane[i - 2] = yrecv[e, 0, f, i].astype(F32)
                plane[ny + i] = yrecv[e, 1, f, i].astype(F32)
            for y in range(ny):
                at = slice(LEAD + y * PITCH, LEAD + y * PITCH + nz)
                if e == 0:
                    t1[f, at] = applied(e, t, f, y, plane, along_x, w_one)
                elif e == 1:
                    t2[f, at] = applied(e, t, f, y, plane, along_x, w_two) - t0[f, at]
                else:
                    doubled = applied(e, t, f, y, plane, along_x, w_two)
                    answer = (c0 * t0[f, at] + c13 * t1[f, at]) + (c2 * plane[y] + c3 * doubled)
                    rounded = answer.astype(BF16)
                    i = f - slot * fields
                    resp[slot, i, y] = rounded
                    dacc[y] += phi[slot, i, y].astype(F32) * rounded.astype(F32)
            return carry

        each(g, field)

    def advance(slot, e):
        per_slot = fields // GROUP

        def group(g, carry):
            step(e, g, slot)
            if e == 0:
                send(1, t1, g)
            elif e == 1:
                send(2, t2, g)
            return carry

        lax.fori_loop(slot * per_slot, (slot + 1) * per_slot, group, 0)

    def begin(slot):
        inner(slot)
        reduce_start(slot)
        partner_halo(slot)

    def expand(slot):
        reduce_finish(slot)
        project(slot)
        advance(slot, 0)

    begin(0)
    if not direct:
        begin(1)
    for slot in range(slots):
        awaited(phi_y.at[slot], early_r.at[slot]).wait()
    for ref, i in ((pert_y, 2), (phi_z, 3), (pert_z, 4)):
        awaited(ref, early_r.at[i]).wait()
    expand(0)
    if direct:
        begin(1)
        advance(0, 1)
        expand(1)
        advance(0, 2)
        advance(1, 1)
    else:
        expand(1)
        advance(0, 1)
        advance(1, 1)
        advance(0, 2)
    advance(1, 2)

    lanes = nx // nka
    lane_at = lax.broadcasted_iota(jnp.int32, (nz, nx), 1)
    scale = 2.0 / (slots * nka)
    block_at = lax.shift_right_logical(lane_at, lanes.bit_length() - 1)
    blocks = [dacc[y] * scale for y in range(ny)]
    stride = nka // 2
    while stride:
        odd = jnp.bitwise_and(block_at, stride) != 0
        for i in range(nka):
            if not i & stride:
                one, two = blocks[i], blocks[i + stride]
                blocks[i] = jnp.where(odd, pltpu.roll(two, stride * lanes, 1), one)
                blocks[i + stride] = jnp.where(odd, two, pltpu.roll(one, nx - stride * lanes, 1))
        stride //= 2
    for d in range(nka):
        dsend[d] = blocks[d]
    den_copies = [
        pltpu.make_async_remote_copy(
            dsend.at[lax.rem(ka + d, nka)], drecv.at[d], den_s, den_r,
            device_id=ka_at(d), device_id_type=MESH,
        )
        for d in range(1, nka)
    ]
    for copy in den_copies:
        copy.start()
    awaited(drecv.at[1:nka], den_r).wait()
    total = dsend[ka]
    for d in range(1, nka):
        total = total + drecv[d]
    dens[...] = jnp.transpose(total)

    awaited(dsend.at[1:nka], den_s).wait()
    for slot in range(slots):
        if not direct:
            awaited(mids[slot].at[1:nka], first_s.at[slot]).wait()
            awaited(lands[slot].at[1:nka], route_s.at[slot]).wait()
        elif shift:
            awaited(lands[slot], route_s.at[slot]).wait()
        awaited(red_recv.at[slot, 1:members], red_s.at[slot]).wait()
        awaited(phi_y.at[slot], early_s.at[slot]).wait()
        awaited(parts_y[slot], early_s.at[5 + slot]).wait()
        awaited(parts_z[slot], early_s.at[7 + slot]).wait()
    for ref, i in ((pert_y, 2), (phi_z, 3), (pert_z, 4)):
        awaited(ref, early_s.at[i]).wait()
    for e in range(1, 3):
        for g in range(slots * fields // GROUP):
            at = pl.ds(g * GROUP, GROUP)
            awaited(ysend.at[e, :, at], halo_s.at[e - 1, g, 0]).wait()
            awaited(zsend.at[e, :, at], halo_s.at[e - 1, g, 1]).wait()


def call(shift, sizes, q_index, orb, coeffs, pot, pert):
    nka, nsy, nsz = sizes
    slots, fields, ny, nz, nx = orb.shape
    count = slots * fields
    groups = count // GROUP
    hbm = pl.BlockSpec(memory_space=pltpu.HBM)
    vmem = pl.BlockSpec(memory_space=pltpu.VMEM)
    dma = pltpu.SemaphoreType.DMA
    t_shape = (count, LEAD + ny * PITCH, nx)
    scratch = [
        pltpu.SMEM(q_index.shape, jnp.int32),
        pltpu.SMEM(coeffs.shape, F32),
        pltpu.VMEM(orb.shape, BF16),
        pltpu.VMEM(orb.shape[1:], BF16),
        pltpu.VMEM(orb.shape[1:], BF16),
        pltpu.VMEM(orb.shape, BF16),
        pltpu.VMEM(orb.shape[1:], BF16),
        pltpu.VMEM(orb.shape[1:], BF16),
        pltpu.VMEM(pot.shape, F32),
        pltpu.VMEM(pot.shape, F32),
        pltpu.VMEM(pot.shape, F32),
        pltpu.VMEM(pot.shape, F32),
        pltpu.VMEM((2 * nx, nx), BF16),
        pltpu.VMEM(t_shape, F32),
        pltpu.VMEM(t_shape, F32),
        pltpu.VMEM(t_shape, F32),
        pltpu.VMEM((40 * 8, nx), F32),
        pltpu.VMEM((nx, nx), F32),
        pltpu.VMEM((32, 8, nx), F32),
        pltpu.VMEM(pot.shape, F32),
        pltpu.VMEM((slots, 2, fields, 2, nz, nx), BF16),
        pltpu.VMEM((2, slots, fields, 2 * ny, nx), BF16),
        pltpu.VMEM((2, slots, fields, 2 * ny, nx), BF16),
        pltpu.VMEM((2, 2, nz, nx), F32),
        pltpu.VMEM((2, 2 * ny, nx), F32),
        pltpu.VMEM((2, 2 * ny, nx), F32),
        pltpu.VMEM((2, fields, 2, nz, nx), BF16),
        pltpu.VMEM((2, fields, 2, nz, nx), BF16),
        pltpu.VMEM((2, fields, 2 * ny, nx), BF16),
        pltpu.VMEM((2, fields, 2 * ny, nx), BF16),
        pltpu.VMEM((slots, 2, fields, 2 * ny, nx), BF16),
        pltpu.VMEM((8 * ny, nx), F32),
        pltpu.VMEM((3, 2, count, 2, nz, nx), BF16),
        pltpu.VMEM((3, 2, count, 2, nz, nx), BF16),
        pltpu.VMEM((3, 2, count, 2 * ny, nx), BF16),
        pltpu.VMEM((3, 2, count, 2 * ny, nx), BF16),
        pltpu.VMEM((slots, 1, nx), F32),
        pltpu.VMEM((slots, nsy * nsz, 1, nx), F32),
        pltpu.VMEM((nka, nz, nx), F32),
        pltpu.VMEM((nka, nz, nx), F32),
        dma((5,)),
        dma((slots,)),
        dma((slots,)),
        dma((slots,)),
        dma((slots,)),
        dma((slots,)),
        dma((slots,)),
        dma((9,)),
        dma((9,)),
        dma((2, groups, 2)),
        dma((2, groups, 2)),
        dma,
        dma,
    ]
    held = [pltpu.with_memory_space_constraint(x, pltpu.HBM) for x in (orb, coeffs, pot, pert)]
    return pl.pallas_call(
        functools.partial(kernel, shift, sizes),
        out_shape=(
            pltpu.VMEM(orb.shape, BF16),
            pltpu.VMEM((nx, nz), F32),
        ),
        in_specs=[pl.BlockSpec(memory_space=pl.ANY)] + [hbm] * 4,
        out_specs=(vmem, vmem),
        scratch_shapes=scratch,
        compiler_params=pltpu.CompilerParams(
            collective_id=1 if shift is None else shift, has_side_effects=True, vmem_limit_bytes=48 << 20
        ),
        name=f"respond_{shift}",
    )(q_index, *held)


def body(sizes, orbitals, coefficients, local_pot, perturb, q_index):
    orb = orbitals.reshape((orbitals.shape[0], -1) + orbitals.shape[3:])
    nka = sizes[0]
    kinds = list(range(0, nka, 2)) + [None]
    branches = [functools.partial(call, kind, sizes) for kind in kinds]
    shift = q_index[0] % nka
    chosen = jnp.where(shift % 2 == 0, shift // 2, len(kinds) - 1)
    responses, density = lax.switch(
        chosen, branches, q_index, orb, coefficients.T, local_pot, perturb
    )
    ny, nz, nx = local_pot.shape
    density = density.reshape((ny, nx // sizes[0], nz)).transpose(0, 2, 1)
    return responses.reshape(orbitals.shape), density


def solution(mesh):
    sizes = (mesh.shape["ka"], mesh.shape["sy"], mesh.shape["sz"])
    return jax.shard_map(
        functools.partial(body, sizes),
        mesh=mesh,
        in_specs=(
            P("ka", None, None, "sy", "sz", None),
            P(),
            P("sy", "sz", None),
            P("sy", "sz", None),
            P(),
        ),
        out_specs=(P("ka", None, None, "sy", "sz", None), P("sy", "sz", "ka")),
        check_vma=False,
    )
```

```python
import functools

import jax
import jax.numpy as jnp
from jax import lax
from jax.experimental import pallas as pl
from jax.experimental.pallas import tpu as pltpu
from jax.sharding import PartitionSpec as P

MESH = pl.DeviceIdType.MESH
F32 = jnp.float32
BF16 = jnp.bfloat16

UNIT = 0.2 * 0.5 / 12.0
EPSILON = 1e-6
BANDS = 4
GROUP = 2
PITCH = 40
LEAD = 8


def fold(value):
    return value[0:8] + value[8:16] + value[16:24] + value[24:32]


def kernel(
    shift, sizes, q_in, orb, coeffs_in, pot, pert, resp, dens,
    q_ref, coeffs, phi, mid_a, mid_b, stage, land_a, land_b, potv, pertv, w_one, w_two, ring, t0, t1, t2, accs, entries, cf, dacc,
    phi_y, phi_z, phi_zs, pert_y, pert_z, pert_zs, part_y_a, part_y_b, part_z_a, part_z_b, part_zs, zpack,
    ysend, yrecv, zsend, zrecv, red_send, red_recv, dsend, drecv,
    load_sem, first_s, first_r, route_s, route_r, red_s, red_r, early_s, early_r, halo_s, halo_r, den_s, den_r,
):
    nka, nsy, nsz = sizes
    slots, fields, ny, nz, nx = phi.shape
    ka, sy, sz = lax.axis_index("ka"), lax.axis_index("sy"), lax.axis_index("sz")

    def ka_at(step):
        return {"ka": lax.rem(ka + step, nka)}

    def group_at(step):
        return {"sy": lax.rem(sy + step // nsz, nsy), "sz": lax.rem(sz + step % nsz, nsz)}

    members = nsy * nsz
    mids, lands = (mid_a, mid_b), (land_a, land_b)
    direct = shift is not None
    parts_y, parts_z = (part_y_a, part_y_b), (part_z_a, part_z_b)
    loads = [
        pltpu.make_async_copy(orb, phi, load_sem.at[0]),
        pltpu.make_async_copy(pert, pertv, load_sem.at[1]),
        pltpu.make_async_copy(pot, potv, load_sem.at[2]),
        pltpu.make_async_copy(coeffs_in, coeffs, load_sem.at[3]),
        pltpu.make_async_copy(q_in, q_ref, load_sem.at[4]),
    ]
    for copy in loads:
        copy.start()

    barrier = pltpu.get_barrier_semaphore()
    peers = [ka_at(d) for d in range(1, nka)] + [group_at(d) for d in range(1, members)]
    for peer in peers:
        pl.semaphore_signal(barrier, inc=1, device_id=peer, device_id_type=MESH)
    pl.semaphore_wait(barrier, len(peers))

    up_y = {"sy": lax.rem(sy + 1, nsy)}
    down_y = {"sy": lax.rem(sy + nsy - 1, nsy)}
    up_z = {"sz": lax.rem(sz + 1, nsz)}
    down_z = {"sz": lax.rem(sz + nsz - 1, nsz)}

    def early(i, high, low, into, peers):
        for src, side, peer in ((high, 0, peers[0]), (low, 1, peers[1])):
            pltpu.make_async_remote_copy(
                src, into.at[side], early_s.at[i], early_r.at[i], device_id=peer, device_id_type=MESH
            ).start()

    along_y, along_z = (up_y, down_y), (up_z, down_z)

    def pack_z(read):
        zpack[...] = read(slice(nz - 8, nz)).astype(F32).reshape(8 * ny, nx)
        high = [zpack[pl.ds(6 + i, ny, stride=8)] for i in range(2)]
        zpack[...] = read(slice(0, 8)).astype(F32).reshape(8 * ny, nx)
        low = [zpack[pl.ds(i, ny, stride=8)] for i in range(2)]
        return jnp.concatenate(high, 0), jnp.concatenate(low, 0)

    def awaited(ref, sem):
        return pltpu.make_async_copy(ref, ref, sem)

    def piece(of):
        return of if direct else jnp.bitwise_and(-q_ref[0] - of, nka - 1)

    def routed(src, dst, send, recv):
        for d in range(1, nka):
            pltpu.make_async_remote_copy(
                src.at[d], dst.at[d], send, recv, device_id=ka_at(d), device_id_type=MESH
            ).start()

    for slot in range(slots):
        if not direct:
            routed(orb.at[slot], mids[slot], first_s.at[slot], first_r.at[slot])
        elif shift:
            pltpu.make_async_remote_copy(
                orb.at[slot], lands[slot], route_s.at[slot], route_r.at[slot],
                device_id=ka_at(nka - shift), device_id_type=MESH,
            ).start()
        else:
            pltpu.make_async_copy(orb.at[slot], lands[slot], route_r.at[slot]).start()

    for slot in range(slots):
        early(slot, orb.at[slot, :, ny - 2 : ny], orb.at[slot, :, 0:2], phi_y.at[slot], along_y)
    early(2, pert.at[ny - 2 : ny], pert.at[0:2], pert_y, along_y)
    for copy in loads:
        copy.wait()
    for slot in range(slots):

        def own_field(i, carry):
            high, low = pack_z(lambda at: phi[slot, i, :, at])
            phi_zs[0, slot, i] = high.astype(BF16)
            phi_zs[1, slot, i] = low.astype(BF16)
            return carry

        lax.fori_loop(0, fields, own_field, 0)
    pert_zs[0], pert_zs[1] = pack_z(lambda at: pertv[:, at])
    early(3, phi_zs.at[0], phi_zs.at[1], phi_z, along_z)
    early(4, pert_zs.at[0], pert_zs.at[1], pert_z, along_z)
    w_one[...] = 0.2 * potv[...] - 0.25
    w_two[...] = 0.4 * potv[...] - 0.5
    dacc[...] = jnp.zeros_like(dacc)

    row_at = lax.broadcasted_iota(jnp.int32, (nx, nx), 0)
    column_at = lax.broadcasted_iota(jnp.int32, (nx, nx), 1)
    apart = jnp.bitwise_and(row_at - column_at, nx - 1)
    circle = jnp.where(
        (apart == 1) | (apart == nx - 1), -16.0, jnp.where((apart == 2) | (apart == nx - 2), 1.0, 0.0)
    ).astype(BF16)
    ring[0:nx] = circle
    ring[nx : 2 * nx] = circle
    ones = jnp.ones((8, nx), BF16)
    entries[...] = jnp.zeros_like(entries)

    if not direct:
        for slot in range(slots):
            mid, land = mids[slot], lands[slot]
            mid[0] = phi[slot, 0]
            awaited(mid.at[1:nka], first_r.at[slot]).wait()
            land[0] = mid[piece(0)]
            for d in range(1, nka):
                stage[slot, d] = mid[piece(d)]
            routed(stage.at[slot], land, route_s.at[slot], route_r.at[slot])

    def inner(slot):
        accs[...] = jnp.zeros_like(accs)

        def plane(y, carry):
            pe = pertv[y]
            source = [
                (pe * phi[slot, 2 * c, y].astype(F32), pe * phi[slot, 2 * c + 1, y].astype(F32))
                for c in range(BANDS)
            ]
            for b in range(BANDS):
                p_re = lands[slot][piece(2 * b), y].astype(F32)
                p_im = lands[slot][piece(2 * b + 1), y].astype(F32)
                at = 8 * (32 + b)
                accs[at : at + 8] += fold(p_re * p_re + p_im * p_im)
                for c in range(BANDS):
                    s_re, s_im = source[c]
                    at = 8 * (b * BANDS + c)
                    accs[at : at + 8] += fold(p_re * s_re + p_im * s_im)
                    at += 8 * 16
                    accs[at : at + 8] += fold(p_re * s_im - p_im * s_re)
            return carry

        landed = lands[slot] if direct else lands[slot].at[1:nka]
        awaited(landed, route_r.at[slot]).wait()
        lax.fori_loop(0, ny, plane, 0)

    def reduce_start(slot):
        count = 32 + BANDS
        summed = accs[pl.ds(0, count, stride=8)]
        for i in range(1, 8):
            summed = summed + accs[pl.ds(i, count, stride=8)]
        entries[0:32] = summed[0:32]
        for b in range(BANDS):
            norm = jnp.broadcast_to(summed[32 + b : 33 + b], (BANDS, nx))
            entries[64 + b * BANDS : 64 + (b + 1) * BANDS] = norm
            entries[80 + b * BANDS : 80 + (b + 1) * BANDS] = norm
        whole = entries[...]
        row = jnp.zeros((8, nx), F32)
        for _ in range(3):
            rounded = whole.astype(BF16)
            row = row + lax.dot_general(
                ones, rounded, (((1,), (1,)), ((), ())), preferred_element_type=F32
            )
            whole = whole - rounded.astype(F32)
        red_send[slot] = row[0:1]
        for d in range(1, members):
            pltpu.make_async_remote_copy(
                red_send.at[slot], red_recv.at[slot, d], red_s.at[slot], red_r.at[slot],
                device_id=group_at(d), device_id_type=MESH,
            ).start()

    def reduce_finish(slot):
        awaited(red_recv.at[slot, 1:members], red_r.at[slot]).wait()
        total = red_send[slot]
        for d in range(1, members):
            total = total + red_recv[slot, d]
        coef = total / (pltpu.roll(total, 64, 1) + EPSILON)
        for i in range(32):
            cf[i] = jnp.broadcast_to(coef[:, i : i + 1], (8, nx))

    def partner_halo(slot):
        land = lands[slot]
        early(5 + slot, land.at[:, ny - 2 : ny], land.at[:, 0:2], parts_y[slot], along_y)

        def field(i, carry):
            high, low = pack_z(lambda at: lands[slot][i, :, at])
            part_zs[slot, 0, i] = high.astype(BF16)
            part_zs[slot, 1, i] = low.astype(BF16)
            return carry

        lax.fori_loop(0, fields, field, 0)
        early(7 + slot, part_zs.at[slot, 0], part_zs.at[slot, 1], parts_z[slot], along_z)

    def projected(pe, own, partner):
        def tiles(value):
            return value.astype(F32).reshape(2, 8, nx)

        pe = tiles(pe)
        partner = [tiles(value) for value in partner]
        out = []
        for c in range(BANDS):
            out_re = pe * tiles(own[2 * c])
            out_im = pe * tiles(own[2 * c + 1])
            for b in range(BANDS):
                c_re = cf[b * BANDS + c]
                c_im = cf[16 + b * BANDS + c]
                p_re, p_im = partner[2 * b], partner[2 * b + 1]
                out_re = out_re - (c_re * p_re - c_im * p_im)
                out_im = out_im - (c_im * p_re + c_re * p_im)
            out += [out_re.reshape(16, nx), out_im.reshape(16, nx)]
        return out

    def project(slot):
        every = range(fields)
        land, part_y, part_z = lands[slot], parts_y[slot], parts_z[slot]
        first_field = slot * fields

        def plane(y, carry):
            for half in range(nz // 16):
                at = pl.ds(16 * half, 16)
                row = pl.ds(pl.multiple_of(LEAD + y * PITCH + 16 * half, 8), 16)
                out = projected(
                    pertv[y, at],
                    [phi[slot, i, y, at] for i in every],
                    [land[piece(i), y, at] for i in every],
                )
                for i in every:
                    t0[first_field + i, row] = out[i]
            return carry

        lax.fori_loop(0, ny, plane, 0)

        def outer_plane(i, carry):
            side, layer = lax.shift_right_logical(i, 1), jnp.bitwise_and(i, 1)
            for half in range(nz // 16):
                at = pl.ds(16 * half, 16)
                out = projected(
                    pert_y[side, layer, at],
                    [phi_y[slot, side, f, layer, at] for f in every],
                    [part_y[side, piece(f), layer, at] for f in every],
                )
                for f in every:
                    yrecv[0, side, first_field + f, layer, at] = out[f].astype(BF16)
            return carry

        def outer_rows(side, carry):
            out = projected(
                pert_z[side],
                [phi_z[side, slot, f] for f in every],
                [part_z[side, piece(f)] for f in every],
            )
            for f in every:
                zrecv[0, side, first_field + f] = out[f].astype(BF16)
            return carry

        awaited(part_y, early_r.at[5 + slot]).wait()
        awaited(part_z, early_r.at[7 + slot]).wait()
        lax.fori_loop(0, 4, outer_plane, 0)
        lax.fori_loop(0, 2, outer_rows, 0)

    def each(g, field):
        def pair(i, carry):
            for j in range(2):
                field(g * GROUP + 2 * i + j, 0)
            return carry

        lax.fori_loop(0, GROUP // 2, pair, 0)

    def halo_copies(e, g):
        at = pl.ds(g * GROUP, GROUP)
        sides = (
            (ysend, yrecv, 0, up_y, 0), (ysend, yrecv, 1, down_y, 0),
            (zsend, zrecv, 0, up_z, 1), (zsend, zrecv, 1, down_z, 1),
        )
        return [
            pltpu.make_async_remote_copy(
                out.at[e, side, at], into.at[e, side, at],
                halo_s.at[e - 1, g, i], halo_r.at[e - 1, g, i], device_id=peer, device_id_type=MESH,
            )
            for out, into, side, peer, i in sides
        ]

    def send(e, t, g):
        def field(f, carry):
            for i in range(2):
                first = LEAD + i * PITCH
                last = LEAD + (ny - 2 + i) * PITCH
                ysend[e, 0, f, i] = t[f, last : last + nz].astype(BF16)
                ysend[e, 1, f, i] = t[f, first : first + nz].astype(BF16)
            high = [t[f, pl.ds(LEAD + nz - 2 + i, ny, stride=PITCH)] for i in range(2)]
            low = [t[f, pl.ds(LEAD + i, ny, stride=PITCH)] for i in range(2)]
            zsend[e, 0, f] = jnp.concatenate(high, 0).astype(BF16)
            zsend[e, 1, f] = jnp.concatenate(low, 0).astype(BF16)
            return carry

        each(g, field)
        for copy in halo_copies(e, g):
            copy.start()

    def applied(e, t, f, y, plane, along_x, w):
        first = LEAD + y * PITCH
        near = plane[y + 1] + plane[y - 1]
        far = plane[y + 2] + plane[y - 2]
        near = near + (t[f, first + 1 : first + 1 + nz] + t[f, first - 1 : first - 1 + nz])
        far = far + (t[f, first + 2 : first + 2 + nz] + t[f, first - 2 : first - 2 + nz])
        unit = UNIT if e == 0 else 2.0 * UNIT
        return w[y] * plane[y] + unit * ((far + along_x[y * nz : (y + 1) * nz]) - 16.0 * near)

    def step(e, g, slot):
        at = pl.ds(g * GROUP, GROUP)
        if e:
            for i, ref in enumerate((yrecv, zrecv)):
                awaited(ref.at[e, :, at], halo_r.at[e - 1, g, i]).wait()
        t = (t0, t1, t2)[e]
        if e == 2:
            row = jnp.bitwise_and(ka + (shift if direct else q_ref[0]), nka - 1) * slots + slot
            c0, c1, c2, c3 = (coeffs[j, row] for j in range(4))
            c13 = c1 - c3

        def field(f, carry):
            for side, start in ((0, LEAD - 2), (1, LEAD + nz)):
                rows_in = zrecv[e, side, f].astype(F32)
                t[f, pl.ds(start, ny, stride=PITCH)] = rows_in[0:ny]
                t[f, pl.ds(start + 1, ny, stride=PITCH)] = rows_in[ny : 2 * ny]
            plane = {}
            for y in range(ny):
                first = LEAD + y * PITCH
                plane[y] = t[f, first : first + nz]
            whole = jnp.concatenate([plane[y] for y in range(ny)], 0)
            high = whole.astype(BF16)
            low = (whole - high.astype(F32)).astype(BF16)
            along_x = jnp.dot(
                jnp.concatenate([high, low], 1), ring[...], preferred_element_type=F32
            )
            for i in range(2):
                plane[i - 2] = yrecv[e, 0, f, i].astype(F32)
                plane[ny + i] = yrecv[e, 1, f, i].astype(F32)
            for y in range(ny):
                at = slice(LEAD + y * PITCH, LEAD + y * PITCH + nz)
                if e == 0:
                    t1[f, at] = applied(e, t, f, y, plane, along_x, w_one)
                elif e == 1:
                    t2[f, at] = applied(e, t, f, y, plane, along_x, w_two) - t0[f, at]
                else:
                    doubled = applied(e, t, f, y, plane, along_x, w_two)
                    answer = (c0 * t0[f, at] + c13 * t1[f, at]) + (c2 * plane[y] + c3 * doubled)
                    rounded = answer.astype(BF16)
                    i = f - slot * fields
                    resp[slot, i, y] = rounded
                    dacc[y] += phi[slot, i, y].astype(F32) * rounded.astype(F32)
            return carry

        each(g, field)

    def advance(slot, e):
        per_slot = fields // GROUP

        def group(g, carry):
            step(e, g, slot)
            if e == 0:
                send(1, t1, g)
            elif e == 1:
                send(2, t2, g)
            return carry

        lax.fori_loop(slot * per_slot, (slot + 1) * per_slot, group, 0)

    def begin(slot):
        inner(slot)
        reduce_start(slot)
        partner_halo(slot)

    def expand(slot):
        reduce_finish(slot)
        project(slot)
        advance(slot, 0)

    begin(0)
    if not direct:
        begin(1)
    for slot in range(slots):
        awaited(phi_y.at[slot], early_r.at[slot]).wait()
    for ref, i in ((pert_y, 2), (phi_z, 3), (pert_z, 4)):
        awaited(ref, early_r.at[i]).wait()
    expand(0)
    if direct:
        begin(1)
        advance(0, 1)
        expand(1)
        advance(0, 2)
        advance(1, 1)
    else:
        expand(1)
        advance(0, 1)
        advance(1, 1)
        advance(0, 2)
    advance(1, 2)

    lanes = nx // nka
    lane_at = lax.broadcasted_iota(jnp.int32, (nz, nx), 1)
    scale = 2.0 / (slots * nka)
    block_at = lax.shift_right_logical(lane_at, lanes.bit_length() - 1)
    blocks = [dacc[y] * scale for y in range(ny)]
    stride = nka // 2
    while stride:
        odd = jnp.bitwise_and(block_at, stride) != 0
        for i in range(nka):
            if not i & stride:
                one, two = blocks[i], blocks[i + stride]
                blocks[i] = jnp.where(odd, pltpu.roll(two, stride * lanes, 1), one)
                blocks[i + stride] = jnp.where(odd, two, pltpu.roll(one, nx - stride * lanes, 1))
        stride //= 2
    for d in range(nka):
        dsend[d] = blocks[d]
    den_copies = [
        pltpu.make_async_remote_copy(
            dsend.at[lax.rem(ka + d, nka)], drecv.at[d], den_s, den_r,
            device_id=ka_at(d), device_id_type=MESH,
        )
        for d in range(1, nka)
    ]
    for copy in den_copies:
        copy.start()
    awaited(drecv.at[1:nka], den_r).wait()
    total = dsend[ka]
    for d in range(1, nka):
        total = total + drecv[d]
    dens[...] = jnp.transpose(total)

    awaited(dsend.at[1:nka], den_s).wait()
    for slot in range(slots):
        if not direct:
            awaited(mids[slot].at[1:nka], first_s.at[slot]).wait()
            awaited(lands[slot].at[1:nka], route_s.at[slot]).wait()
        elif shift:
            awaited(lands[slot], route_s.at[slot]).wait()
        awaited(red_recv.at[slot, 1:members], red_s.at[slot]).wait()
        awaited(phi_y.at[slot], early_s.at[slot]).wait()
        awaited(parts_y[slot], early_s.at[5 + slot]).wait()
        awaited(parts_z[slot], early_s.at[7 + slot]).wait()
    for ref, i in ((pert_y, 2), (phi_z, 3), (pert_z, 4)):
        awaited(ref, early_s.at[i]).wait()
    for e in range(1, 3):
        for g in range(slots * fields // GROUP):
            at = pl.ds(g * GROUP, GROUP)
            awaited(ysend.at[e, :, at], halo_s.at[e - 1, g, 0]).wait()
            awaited(zsend.at[e, :, at], halo_s.at[e - 1, g, 1]).wait()


def call(shift, sizes, q_index, orb, coeffs, pot, pert):
    nka, nsy, nsz = sizes
    slots, fields, ny, nz, nx = orb.shape
    count = slots * fields
    groups = count // GROUP
    hbm = pl.BlockSpec(memory_space=pltpu.HBM)
    vmem = pl.BlockSpec(memory_space=pltpu.VMEM)
    dma = pltpu.SemaphoreType.DMA
    t_shape = (count, LEAD + ny * PITCH, nx)
    scratch = [
        pltpu.SMEM(q_index.shape, jnp.int32),
        pltpu.SMEM(coeffs.shape, F32),
        pltpu.VMEM(orb.shape, BF16),
        pltpu.VMEM(orb.shape[1:], BF16),
        pltpu.VMEM(orb.shape[1:], BF16),
        pltpu.VMEM(orb.shape, BF16),
        pltpu.VMEM(orb.shape[1:], BF16),
        pltpu.VMEM(orb.shape[1:], BF16),
        pltpu.VMEM(pot.shape, F32),
        pltpu.VMEM(pot.shape, F32),
        pltpu.VMEM(pot.shape, F32),
        pltpu.VMEM(pot.shape, F32),
        pltpu.VMEM((2 * nx, nx), BF16),
        pltpu.VMEM(t_shape, F32),
        pltpu.VMEM(t_shape, F32),
        pltpu.VMEM(t_shape, F32),
        pltpu.VMEM((40 * 8, nx), F32),
        pltpu.VMEM((nx, nx), F32),
        pltpu.VMEM((32, 8, nx), F32),
        pltpu.VMEM(pot.shape, F32),
        pltpu.VMEM((slots, 2, fields, 2, nz, nx), BF16),
        pltpu.VMEM((2, slots, fields, 2 * ny, nx), BF16),
        pltpu.VMEM((2, slots, fields, 2 * ny, nx), BF16),
        pltpu.VMEM((2, 2, nz, nx), F32),
        pltpu.VMEM((2, 2 * ny, nx), F32),
        pltpu.VMEM((2, 2 * ny, nx), F32),
        pltpu.VMEM((2, fields, 2, nz, nx), BF16),
        pltpu.VMEM((2, fields, 2, nz, nx), BF16),
        pltpu.VMEM((2, fields, 2 * ny, nx), BF16),
        pltpu.VMEM((2, fields, 2 * ny, nx), BF16),
        pltpu.VMEM((slots, 2, fields, 2 * ny, nx), BF16),
        pltpu.VMEM((8 * ny, nx), F32),
        pltpu.VMEM((3, 2, count, 2, nz, nx), BF16),
        pltpu.VMEM((3, 2, count, 2, nz, nx), BF16),
        pltpu.VMEM((3, 2, count, 2 * ny, nx), BF16),
        pltpu.VMEM((3, 2, count, 2 * ny, nx), BF16),
        pltpu.VMEM((slots, 1, nx), F32),
        pltpu.VMEM((slots, nsy * nsz, 1, nx), F32),
        pltpu.VMEM((nka, nz, nx), F32),
        pltpu.VMEM((nka, nz, nx), F32),
        dma((5,)),
        dma((slots,)),
        dma((slots,)),
        dma((slots,)),
        dma((slots,)),
        dma((slots,)),
        dma((slots,)),
        dma((9,)),
        dma((9,)),
        dma((2, groups, 2)),
        dma((2, groups, 2)),
        dma,
        dma,
    ]
    held = [pltpu.with_memory_space_constraint(x, pltpu.HBM) for x in (orb, coeffs, pot, pert)]
    return pl.pallas_call(
        functools.partial(kernel, shift, sizes),
        out_shape=(
            pltpu.VMEM(orb.shape, BF16),
            pltpu.VMEM((nx, nz), F32),
        ),
        in_specs=[pl.BlockSpec(memory_space=pl.ANY)] + [hbm] * 4,
        out_specs=(vmem, vmem),
        scratch_shapes=scratch,
        compiler_params=pltpu.CompilerParams(
            collective_id=1 if shift is None else shift, has_side_effects=True, vmem_limit_bytes=48 << 20
        ),
        name=f"respond_{shift}",
    )(q_index, *held)


def body(sizes, orbitals, coefficients, local_pot, perturb, q_index):
    orb = orbitals.reshape((orbitals.shape[0], -1) + orbitals.shape[3:])
    nka = sizes[0]
    kinds = list(range(0, nka, 2)) + [None]
    branches = [functools.partial(call, kind, sizes) for kind in kinds]
    shift = q_index[0] % nka
    chosen = jnp.where(shift % 2 == 0, shift // 2, len(kinds) - 1)
    responses, density = lax.switch(
        chosen, branches, q_index, orb, coefficients.T, local_pot, perturb
    )
    ny, nz, nx = local_pot.shape
    density = density.reshape((ny, nx // sizes[0], nz)).transpose(0, 2, 1)
    return responses.reshape(orbitals.shape), density


def solution(mesh):
    sizes = (mesh.shape["ka"], mesh.shape["sy"], mesh.shape["sz"])
    return jax.shard_map(
        functools.partial(body, sizes),
        mesh=mesh,
        in_specs=(
            P("ka", None, None, "sy", "sz", None),
            P(),
            P("sy", "sz", None),
            P("sy", "sz", None),
            P(),
        ),
        out_specs=(P("ka", None, None, "sy", "sz", None), P("sy", "sz", "ka")),
        check_vma=False,
    )
```
